32 devices in a mesh: groups: 2 (over x), gy: 8 (over z, y), gz: 2 (over core).
Axes of the slice: x: 2, y: 2, z: 4, core: 2. Of those that a mesh axis runs over, the one named last changes fastest.
Arguments:
- nodes: bfloat16 [32768, 512], P(('groups', 'gy', 'gz')), parts along dimension 0, may hold values from -6 to 6
- block_mask: int32 [256, 8], P(('groups', 'gy', 'gz')), parts along dimension 0, may hold values 0 or 1
- border_ids: int32 [4096], P(('groups', 'gy', 'gz')), parts along dimension 0, may hold values from 0 to 1023
- contact: bfloat16 [16384, 128], P(('groups', 'gy', 'gz')), parts along dimension 0, may hold values from -6 to 6
- edge_source: int32 [16384], P(('groups', 'gy', 'gz')), parts along dimension 0, may hold values from 0 to 1023
- edge_target: int32 [16384], P(('groups', 'gy', 'gz')), parts along dimension 0, may hold values from 0 to 1023
- edge_owner: int32 [16384, 1], P(('groups', 'gy', 'gz')), parts along dimension 0, may hold values from 0 to 15; in each aligned block of 512 rows (0 to 511, 512 to 1023, ...) at most 64 rows name the same one
- norm_gain: float32 [512], replicated, may hold values from 0.1 to 1.9
- w_qkv: bfloat16 [512, 1536], replicated, may hold values from -1 to 1
- w_attn_out: bfloat16 [512, 512], replicated, may hold values from -0.25 to 0.25
- w_source: bfloat16 [512, 512], replicated, may hold values from -0.25 to 0.25
- w_target: bfloat16 [512, 512], replicated, may hold values from -0.25 to 0.25
- w_contact: bfloat16 [128, 512], replicated, may hold values from -0.5 to 0.5
- w_score: float32 [512], replicated, may hold values from -0.25 to 0.25
Outputs:
- node_state: bfloat16 [32768, 512], P(('groups', 'gy', 'gz')), parts along dimension 0
- edge_scores: float32 [16384], P(('groups', 'gy', 'gz')), parts along dimension 0
The draws below stay inside these ranges and needn't reach their ends.
There are 2 independent parts, one for each index of `groups`. The reference program is written for one: setup_inputs(seed, part) draws one part's arguments, and reference() takes and returns one part's arrays. A program takes and returns all parts, laid end to end along the dimension named above; an argument that names none is the same for every part. Nothing has to cross between parts.
Inputs may be any that keep to these rules, and one draw needn't show every extreme that they name: `edge_owner`: among the edges of one brick, no brick is named by more than 64 of them, a bound that some block reaches.
All inputs are finite; a program needn't handle non-finite values. No bound on the sum of `block_mask` on one device may be relied on, other than what follows from the above.
Results may differ from the reference program's by a relative error of at most 0.011.
Values may be sent and summed in bfloat16 or wider, within the bound.
No kernel may reach another device: no remote copies, remote signals or barrier semaphores. Data moves between devices by JAX's collectives and lax.ppermute only.
A program may use at most 128 MiB of HBM per device.

```python
import math
import jax
import jax.numpy as jnp
import numpy as np
from jax import lax

D = 512
HEADS = 8
HEAD_DIM = 64
HIDDEN_SIZE = 512
PANEL = 128
BLOCK = 128
S_DEV = 1024
E_DEV = 512
BORDER = 128
NB = 8
CAP = 64
NODES = 16384
EDGES = 8192
BORDERS = 2048
N_GY = 8
N_GZ = 2


def draw_w_qkv(key, part):
    key_base = jax.random.fold_in(key, 11)
    result = jax.random.normal(key_base, (D, 3 * D), jnp.float32) * D ** (-0.5)
    return jnp.clip(result, -1.0, 1.0).astype(jnp.bfloat16)


def set_ends(drawn, key, low, top_value):
    shape = drawn.shape
    index_at = [jax.random.randint(jax.random.fold_in(key, axis), (), 0, shape[axis]) for axis in range(len(shape))]
    drawn = drawn.at[tuple(index_at)].set(low)
    longest = shape.index(max(shape))
    index_at[longest] = (index_at[longest] + 1) % shape[longest]
    return drawn.at[tuple(index_at)].set(top_value)


def level_of(rng, extent, shards, least, largest):
    loudness, own = 1.0, jax.random.fold_in(rng, 6)
    for dim, blocks in shards:
        heights = jnp.exp(jax.random.uniform(jax.random.fold_in(own, dim), (blocks,), jnp.float32, least / len(shards), largest / len(shards)))
        loudness = loudness * jnp.repeat(heights, extent[dim] // blocks).reshape([-1 if axis == dim else 1 for axis in range(len(extent))])
    return loudness


def deal_out(own_key, own, number, rows, number_of, top, bound, lean):
    ranking = jax.random.permutation(own_key, number_of)
    packed, common = shares(number_of, rows * top, bound, lean, True), shares(number_of, rows * top, bound, lean, False)
    places = jnp.arange(number_of)

    def named(tallies, rotation):
        used = int((tallies > 0).sum())
        fixed = max(1, used // 4)
        moved = fixed + (places - fixed + rotation * (used - fixed)) % max(1, number_of - fixed)
        return jnp.zeros((number_of,), jnp.int32).at[ranking[jnp.where(places < fixed, places, moved)]].set(jnp.asarray(tallies, jnp.int32))

    tallies = jnp.where(number % 4 == 0, named(packed, number // 4), named(common, number - number // 4 - 1))
    mixed = jax.random.permutation(jax.random.fold_in(own, 3), number_of)
    donor, sink = mixed[0:number_of // 2 * 2:2], mixed[1:number_of // 2 * 2:2]
    slack = jnp.minimum(tallies[donor] - 1, bound - tallies[sink]) // 2
    slack = jnp.where((donor == ranking[0]) | (sink == ranking[0]) | (tallies[sink] == 0), 0, jnp.maximum(slack, 0))
    moved = jax.random.randint(jax.random.fold_in(own, 4), (number_of // 2,), 0, 1 << 20) % (slack + 1)
    tallies = tallies.at[donor].add(-moved).at[sink].add(moved)
    labels = jnp.searchsorted(jnp.cumsum(tallies), jnp.arange(rows * top), side="right").astype(jnp.int32)
    table = labels.reshape(top, rows).T
    table = table[jax.random.permutation(jax.random.fold_in(own, 1), rows)]
    rotation = jax.random.randint(jax.random.fold_in(own, 2), (rows, 1), 0, top)
    return jnp.take_along_axis(table, (jnp.arange(top)[None, :] + rotation) % top, axis=1)


def shares(amount, total, bound, slope, full):
    portions = [(1 << 20) // math.isqrt(grade ** slope) + 1 for grade in range(1, amount + 1)]
    largest = bound if full else min(bound, max(-(-total // amount), total * portions[0] // sum(portions)))
    least = 1 if total - largest >= amount - 1 else 0
    holding, rest = [largest] + [least] * (amount - 1), total - largest - least * (amount - 1)
    while rest > 0:
        free = [i for i in range(1, amount) if holding[i] < largest] or [i for i in range(1, amount) if holding[i] < bound]
        whole, remaining = sum([portions[i] for i in free]), rest
        for i in free:
            extra = min(bound - holding[i], max(1, remaining * portions[i] // whole), rest)
            holding[i] = holding[i] + extra
            rest = rest - extra
    return np.array(holding)


def centred(own_key, shape, scale, most, split=(), held_as=jnp.bfloat16):
    values = jax.random.normal(own_key, shape, jnp.float32) * scale
    if len(split) > 0:
        values = level_of(own_key, shape, split, -0.22, 0.18) * values
    return jnp.clip(values, min=-most, max=most).astype(held_as)


def setup_inputs(seed: int = 0, part: int = 0) -> dict:
    key_of = jax.random.split(jax.random.key(seed), 15)
    own_keys = jax.random.split(jax.random.fold_in(key_of[14], part), 15)
    nodes = centred(own_keys[0], (NODES, D), 1.0, 6.0, ((0, 16),))
    block_mask = set_ends((jax.random.randint(own_keys[1], (NODES // BLOCK, NB), 0, 3) < 1).astype(jnp.int32), jax.random.fold_in(own_keys[1], 1), 0, 1)
    border_ids = set_ends(jax.random.randint(own_keys[2], (BORDERS,), 0, S_DEV), jax.random.fold_in(own_keys[2], 1), 0, S_DEV - 1).astype(jnp.int32)
    contact = centred(own_keys[3], (EDGES, PANEL), 1.0, 6.0, ((0, 16),))
    edge_source = set_ends(jax.random.randint(own_keys[4], (EDGES,), 0, S_DEV), jax.random.fold_in(own_keys[4], 1), 0, S_DEV - 1).astype(jnp.int32)
    edge_target = set_ends(jax.random.randint(own_keys[5], (EDGES,), 0, S_DEV), jax.random.fold_in(own_keys[5], 1), 0, S_DEV - 1).astype(jnp.int32)
    edge_owner_keys = jax.random.split(jax.random.fold_in(own_keys[6], 1), EDGES // E_DEV)
    edge_owner_turns = jax.random.permutation(jax.random.fold_in(own_keys[6], 3), EDGES // E_DEV)
    edge_owner = jax.vmap(lambda own, number: deal_out(jax.random.fold_in(own_keys[6], 2), own, number, E_DEV, N_GY * N_GZ, 1, CAP, 2))(edge_owner_keys, edge_owner_turns).reshape((EDGES, 1))
    norm_gain = jnp.clip(1.0 + 0.18 * jax.random.normal(key_of[7], (D,), jnp.float32), 0.1, 1.9)
    w_qkv = draw_w_qkv(jax.random.fold_in(key_of[14], 71), part)
    w_attn_out = centred(key_of[9], (D, D), D ** -0.5, 0.25)
    w_source = centred(key_of[10], (D, HIDDEN_SIZE), D ** -0.5, 0.25)
    w_target = centred(key_of[11], (D, HIDDEN_SIZE), D ** -0.5, 0.25)
    w_contact = centred(key_of[12], (PANEL, HIDDEN_SIZE), PANEL ** -0.5, 0.5)
    w_score = centred(key_of[13], (HIDDEN_SIZE,), HIDDEN_SIZE ** -0.5, 0.25, (), jnp.float32)
    return {"nodes": nodes, "block_mask": block_mask, "border_ids": border_ids, "contact": contact, "edge_source": edge_source, "edge_target": edge_target, "edge_owner": edge_owner, "norm_gain": norm_gain, "w_qkv": w_qkv, "w_attn_out": w_attn_out, "w_source": w_source, "w_target": w_target, "w_contact": w_contact, "w_score": w_score}


def rms_norm(values, gain):
    wide = values.astype(jnp.float32)
    return wide * lax.rsqrt(lax.optimization_barrier(jnp.mean(wide * wide, axis=-1, keepdims=True)) + 1e-06) * gain

def attend(queries, keys, values, halo_keys, halo_values, blocks, valid):
    rows = queries.shape[0]
    width = queries.shape[1]
    span = min(512, rows)
    all_keys = jnp.concatenate([keys, halo_keys], 0).astype(jnp.float32)
    all_values = jnp.concatenate([values, halo_values], 0).astype(jnp.float32)
    count = all_keys.shape[0]
    key_heads = all_keys.reshape(count, HEADS, -1)
    value_heads = all_values.reshape(count, HEADS, -1)
    key_block = jnp.arange(rows) // BLOCK
    halo_allowed = jnp.repeat(valid, halo_keys.shape[0] // 4) > 0

    def attend_rows(start):
        query_rows = lax.dynamic_slice_in_dim(queries, start, span, 0).astype(jnp.float32).reshape(span, HEADS, -1)
        scores = jnp.einsum('qhd,khd->hqk', query_rows, key_heads) * (1.0 / HEAD_DIM ** 0.5)
        row_block = (start + jnp.arange(span)) // BLOCK
        local_allowed = jnp.repeat(jnp.take(blocks, row_block, axis=0) > 0, BLOCK, axis=1)
        local_allowed = local_allowed | (row_block[:, None] == key_block[None, :])
        allowed = jnp.concatenate([local_allowed, jnp.broadcast_to(halo_allowed[None, :], (span, halo_allowed.shape[0]))], 1)
        scores = jnp.where(allowed[None], scores, -1e+30)
        row_max = lax.optimization_barrier(jnp.max(scores, axis=-1, keepdims=True))
        weights = jnp.exp(scores - row_max)
        totals = lax.optimization_barrier(jnp.sum(weights, axis=-1))
        weights_bf = weights.astype(jnp.bfloat16).astype(jnp.float32)
        mixed = jnp.einsum('hqk,khd->qhd', weights_bf, value_heads) / jnp.transpose(totals)[:, :, None]
        return mixed.reshape(span, width).astype(jnp.bfloat16)
    starts = jnp.arange(rows // span) * span
    return lax.map(attend_rows, starts).reshape(rows, width)

def reference(nodes, block_mask, border_ids, contact, edge_source, edge_target, edge_owner, norm_gain, w_qkv, w_attn_out, w_source, w_target, w_contact, w_score):
    bricks = N_GY * N_GZ
    normed = rms_norm(nodes, norm_gain).astype(jnp.bfloat16)
    qkv = jnp.dot(normed, w_qkv, preferred_element_type=jnp.float32).astype(jnp.bfloat16)
    queries = qkv[:, :D].reshape(bricks, S_DEV, D)
    keys_values = qkv[:, D:].reshape(bricks, S_DEV, 2 * D)
    border_local = border_ids.reshape(bricks, BORDER)
    borders = jax.vmap(lambda table, picks: jnp.take(table, picks, axis=0))(keys_values, border_local)
    blocks_all = block_mask.reshape(bricks, NB, NB)

    def per_brick(brick):
        y_index = brick // N_GZ
        z_index = brick % N_GZ
        y_down = jnp.clip(brick - N_GZ, 0, bricks - 1)
        y_up = jnp.clip(brick + N_GZ, 0, bricks - 1)
        z_down = jnp.clip(brick - 1, 0, bricks - 1)
        z_up = jnp.clip(brick + 1, 0, bricks - 1)
        valid = jnp.stack([y_index > 0, y_index < N_GY - 1, z_index > 0, z_index < N_GZ - 1]).astype(jnp.float32)
        halo = jnp.concatenate([borders[y_down], borders[y_up], borders[z_down], borders[z_up]], 0)
        own = keys_values[brick]
        return attend(queries[brick], own[:, :D], own[:, D:], halo[:, :D], halo[:, D:], blocks_all[brick], valid)
    attended = lax.map(per_brick, jnp.arange(bricks)).reshape(NODES, D)
    state = nodes.astype(jnp.float32) + jnp.dot(attended, w_attn_out, preferred_element_type=jnp.float32)
    node_state = state.astype(jnp.bfloat16)
    source_table = jnp.dot(node_state, w_source, preferred_element_type=jnp.float32).astype(jnp.bfloat16)
    target_table = jnp.dot(node_state, w_target, preferred_element_type=jnp.float32).astype(jnp.bfloat16)
    owner = edge_owner[:, 0]
    source_global = (jnp.arange(EDGES) // E_DEV).astype(jnp.int32) * S_DEV + edge_source
    target_global = owner * S_DEV + edge_target
    pre = jnp.take(source_table, source_global, axis=0).astype(jnp.float32)
    pre = pre + jnp.take(target_table, target_global, axis=0).astype(jnp.float32)
    pre = pre + jnp.dot(contact, w_contact, preferred_element_type=jnp.float32)
    edge_scores = jnp.dot(jax.nn.gelu(pre), w_score, precision=lax.Precision.HIGHEST)
    return (node_state, edge_scores)
```

```python
import functools

import jax
import jax.numpy as jnp
from jax import lax
from jax.experimental import pallas as pl
from jax.experimental.pallas import tpu as pltpu
from jax.sharding import PartitionSpec as P

HEADS = 8
HEAD_DIM = 64
BLOCK = 128
PAIR = 2 * HEAD_DIM
SPAN = 256
F32 = jnp.float32
BF16 = jnp.bfloat16
NT = (((1,), (1,)), ((), ()))


def dot(lhs, rhs):
    return jnp.dot(lhs, rhs, preferred_element_type=F32)


def dot_nt(lhs, rhs):
    return lax.dot_general(lhs, rhs, NT, preferred_element_type=F32)


def ones_where(condition):
    return jnp.where(condition, 1.0, 0.0).astype(BF16)


def iota(shape, axis):
    return lax.broadcasted_iota(jnp.int32, shape, axis)


def columns_of(rows):
    count, lanes = rows.shape
    if count < 8:
        rows = jnp.concatenate([rows] * (8 // count), 0)
    return jnp.transpose(rows)


def picked(index_rows, table):
    count = index_rows.shape[0]
    columns = columns_of(index_rows)
    lanes = iota((128, table.shape[0]), 1)
    hot = [ones_where(columns[:, r : r + 1] == lanes) for r in range(count)]
    return dot(jnp.concatenate(hot, 0), table)


def normed_rows(values, gain):
    wide = values.astype(F32)
    mean = jnp.mean(wide * wide, axis=-1, keepdims=True)
    return (wide * lax.rsqrt(mean + 1e-06) * gain).astype(BF16)


def prepare(ids_ref, owner_ref, target_ref, nodes_ref, border_ref, request_ref, place_ref):
    bricks, capacity = request_ref.shape
    edges = owner_ref.shape[1]
    border_ref[...] = picked(ids_ref[...], nodes_ref[...]).astype(BF16)
    owner = owner_ref[...]
    target = target_ref[...]
    mine = iota((bricks, edges), 0) == owner
    mine_f = jnp.where(mine, 1.0, 0.0)
    before = ones_where(iota((edges, edges), 0) < iota((edges, edges), 1))
    counts = dot(mine_f.astype(BF16), before)
    slots = jnp.sum(counts * mine_f, axis=0, keepdims=True).astype(jnp.int32)
    place = owner * capacity + slots
    for r in range(edges // 128):
        place_ref[r : r + 1, :] = place[:, r * 128 : (r + 1) * 128]
    at_slot = ones_where(iota((capacity, edges), 0) == slots)
    high = (mine_f * (target >> 5).astype(F32)).astype(BF16)
    low = (mine_f * (target & 31).astype(F32)).astype(BF16)
    request = dot_nt(high, at_slot) * 32.0 + dot_nt(low, at_slot)
    request_ref[...] = request.astype(jnp.int32)


def project(nodes_ref, gain_ref, w_ref, qkv_ref):
    normed = normed_rows(nodes_ref[...], gain_ref[...])
    qkv_ref[...] = dot(normed, w_ref[...]).astype(BF16)


def attend(
    nodes_ref,
    q_ref,
    kv_ref,
    halo_ref,
    bias_ref,
    gain_ref,
    w_kv_ref,
    w_out_ref,
    w_source_ref,
    w_target_ref,
    state_ref,
    source_ref,
    target_ref,
    k_ref,
    v_ref,
):
    rows, width = kv_ref.shape[0], q_ref.shape[1]
    keys = k_ref.shape[0]
    span = q_ref.shape[0]
    step = pl.program_id(0)
    low_lanes = iota((keys, PAIR), 1) < HEAD_DIM

    @pl.when(step == 0)
    def _():
        halo = dot(normed_rows(halo_ref[...], gain_ref[...]), w_kv_ref[...]).astype(BF16)
        k_ref[:rows, :] = kv_ref[:, :width]
        k_ref[rows:, :] = halo[:, :width]
        for pair in range(width // PAIR):
            at = slice(pair * PAIR, (pair + 1) * PAIR)
            v_at = slice(width + pair * PAIR, width + (pair + 1) * PAIR)
            values = jnp.concatenate([kv_ref[:, v_at], halo[:, v_at]], 0)
            one = jnp.ones_like(values)
            v_ref[2 * pair] = jnp.where(low_lanes, values, one)
            v_ref[2 * pair + 1] = jnp.where(low_lanes, one, values)

    block = (step * span + iota((span, 128), 0)) // BLOCK
    q_block = ones_where(block == iota((span, 128), 1))
    bias = bias_ref[...]
    scale = 1.4426950408889634 / HEAD_DIM**0.5
    low = iota((span, PAIR), 1) < HEAD_DIM
    attended = []
    for pair in range(width // PAIR):
        at = slice(pair * PAIR, (pair + 1) * PAIR)
        q_pair = q_ref[:, at]
        k_pair = jnp.concatenate([k_ref[:, at], bias], 1)
        mixed = []
        for half in range(2):
            q_own = jnp.where(low if half == 0 else ~low, q_pair, jnp.zeros_like(q_pair))
            scores = dot_nt(jnp.concatenate([q_own, q_block], 1), k_pair)
            top = jnp.max(scores, axis=1, keepdims=True) * scale
            weights = jnp.exp2((scores * scale - top).astype(BF16))
            mixed.append(dot(weights, v_ref[2 * pair + half]))
        total = pltpu.roll(jnp.where(low, mixed[1], mixed[0]), HEAD_DIM, 1)
        attended.append((jnp.where(low, mixed[0], mixed[1]) / total).astype(BF16))
    state = nodes_ref[...].astype(F32) + dot(jnp.concatenate(attended, 1), w_out_ref[...])
    state = state.astype(BF16)
    state_ref[...] = state
    source_ref[...] = dot(state, w_source_ref[...]).astype(BF16)
    target_ref[...] = dot(state, w_target_ref[...]).astype(BF16)


def answer(request_ref, table_ref, out_ref):
    out_ref[...] = picked(request_ref[...], table_ref[...]).astype(BF16)


def own_part(index_ref, table_ref, contact_ref, w_ref, out_ref):
    out_ref[...] = picked(index_ref[...], table_ref[...]) + dot(contact_ref[...], w_ref[...])


def score(place_ref, answers_ref, part_ref, w_ref, out_ref):
    pre = part_ref[...] + picked(place_ref[...], answers_ref[...])
    weighted = jax.nn.gelu(pre) * w_ref[...]
    folded = weighted[:, :128]
    for at in range(128, weighted.shape[1], 128):
        folded = folded + weighted[:, at : at + 128]
    out_ref[...] = jnp.sum(jnp.transpose(folded), axis=0, keepdims=True)


def shape(dims, dtype):
    return jax.ShapeDtypeStruct(dims, dtype)


def neighbours(block):
    pieces, valid = [], []
    for axis in ("gy", "gz"):
        count = lax.axis_size(axis)
        index = lax.axis_index(axis)
        if count == 2:
            pieces.append(lax.ppermute(block, axis, [(0, 1), (1, 0)]))
            valid.append(jnp.bool_(True))
        elif count > 2:
            forward = [(i, i + 1) for i in range(count - 1)]
            backward = [(target, source) for source, target in forward]
            pieces.append(lax.ppermute(block, axis, forward))
            valid.append(index > 0)
            pieces.append(lax.ppermute(block, axis, backward))
            valid.append(index < count - 1)
    return jnp.concatenate(pieces, 0), jnp.stack(valid)


def local(
    nodes,
    block_mask,
    border_ids,
    contact,
    edge_source,
    edge_target,
    edge_owner,
    norm_gain,
    w_qkv,
    w_attn_out,
    w_source,
    w_target,
    w_contact,
    w_score,
):
    rows, width = nodes.shape
    edges = edge_source.shape[0]
    border_count = border_ids.shape[0]
    bricks = lax.axis_size("gy") * lax.axis_size("gz")
    capacity = max(2 * edges // bricks, 2)
    vmem = pltpu.CompilerParams(vmem_limit_bytes=60 * 1024 * 1024)

    border, request, place = pl.pallas_call(
        prepare,
        out_shape=(
            shape((border_count, width), BF16),
            shape((bricks, capacity), jnp.int32),
            shape((edges // 128, 128), jnp.int32),
        ),
        compiler_params=vmem,
    )(
        border_ids.reshape(border_count // 128, 128),
        edge_owner.reshape(1, edges),
        edge_target.reshape(1, edges),
        nodes,
    )
    halo, valid = neighbours(border)
    requests = lax.all_gather(request, ("gy", "gz"))
    me = lax.axis_index("gy") * lax.axis_size("gz") + lax.axis_index("gz")
    asked = lax.dynamic_index_in_dim(requests, me, 1, keepdims=False)
    asked = asked.reshape(bricks * capacity // 128, 128)

    gain = norm_gain.reshape(1, width)
    qkv = pl.pallas_call(
        project,
        out_shape=shape((rows, 3 * width), BF16),
        grid=(rows // SPAN,),
        in_specs=[
            pl.BlockSpec((SPAN, width), lambda i: (i, 0)),
            pl.BlockSpec((1, width), lambda i: (0, 0)),
            pl.BlockSpec((width, 3 * width), lambda i: (0, 0)),
        ],
        out_specs=pl.BlockSpec((SPAN, 3 * width), lambda i: (i, 0)),
        compiler_params=vmem,
    )(nodes, gain, w_qkv)

    blocks = rows // BLOCK
    seen = (block_mask > 0) | jnp.eye(blocks, dtype=jnp.bool_)
    seen = jnp.concatenate(
        [seen, jnp.broadcast_to(valid[None, :], (blocks, valid.shape[0]))], 1
    )
    seen = jnp.pad(seen.T, ((0, 0), (0, 128 - blocks)))
    bias = jnp.repeat(jnp.where(seen, 0.0, -1e30).astype(BF16), BLOCK, axis=0)
    keys = rows + halo.shape[0]

    def fixed(dims, at=(0, 0)):
        return pl.BlockSpec(dims, lambda i: at)

    def tiled(dims):
        return pl.BlockSpec(dims, lambda i: (i, 0))

    node_state, source_table, target_table = pl.pallas_call(
        attend,
        out_shape=(shape((rows, width), BF16),) * 3,
        grid=(rows // SPAN,),
        in_specs=[
            tiled((SPAN, width)),
            tiled((SPAN, width)),
            fixed((rows, 2 * width)),
            fixed((halo.shape[0], width)),
            fixed((keys, 128)),
            fixed((1, width)),
            fixed((width, 2 * width)),
            fixed((width, width)),
            fixed((width, width)),
            fixed((width, width)),
        ],
        out_specs=(tiled((SPAN, width)),) * 3,
        scratch_shapes=[
            pltpu.VMEM((keys, width), BF16),
            pltpu.VMEM((HEADS, keys, PAIR), BF16),
        ],
        compiler_params=vmem,
    )(
        nodes,
        qkv[:, :width],
        qkv[:, width:],
        halo,
        bias,
        gain,
        w_qkv[:, width:],
        w_attn_out,
        w_source,
        w_target,
    )

    hidden = w_target.shape[1]
    answers = pl.pallas_call(
        answer, out_shape=shape((bricks * capacity, hidden), BF16), compiler_params=vmem
    )(asked, target_table)
    answers = lax.all_to_all(
        answers.reshape(bricks, capacity, hidden),
        ("gy", "gz"),
        split_axis=0,
        concat_axis=0,
        tiled=True,
    ).reshape(bricks * capacity, hidden)
    part = pl.pallas_call(
        own_part, out_shape=shape((edges, hidden), F32), compiler_params=vmem
    )(edge_source.reshape(edges // 128, 128), source_table, contact, w_contact)
    scores = pl.pallas_call(score, out_shape=shape((1, edges), F32), compiler_params=vmem)(
        place, answers, part, w_score.reshape(1, hidden)
    )
    return (node_state, scores.reshape(edges))


def solution(mesh):
    split = ("groups", "gy", "gz")
    in_specs = (
        P(split, None),
        P(split, None),
        P(split),
        P(split, None),
        P(split),
        P(split),
        P(split, None),
        P(),
        P(),
        P(),
        P(),
        P(),
        P(),
        P(),
    )
    out_specs = (P(split, None), P(split))
    return jax.shard_map(local, mesh=mesh, in_specs=in_specs, out_specs=out_specs, check_vma=False)
```

```python
import functools

import jax
import jax.numpy as jnp
from jax import lax
from jax.experimental import pallas as pl
from jax.experimental.pallas import tpu as pltpu
from jax.sharding import PartitionSpec as P

HEADS = 8
HEAD_DIM = 64
BLOCK = 128
PAIR = 2 * HEAD_DIM
SPAN = 256
F32 = jnp.float32
BF16 = jnp.bfloat16
NT = (((1,), (1,)), ((), ()))


def dot(lhs, rhs):
    return jnp.dot(lhs, rhs, preferred_element_type=F32)


def dot_nt(lhs, rhs):
    return lax.dot_general(lhs, rhs, NT, preferred_element_type=F32)


def ones_where(condition):
    return jnp.where(condition, 1.0, 0.0).astype(BF16)


def iota(shape, axis):
    return lax.broadcasted_iota(jnp.int32, shape, axis)


def columns_of(rows):
    count, lanes = rows.shape
    if count < 8:
        rows = jnp.concatenate([rows] * (8 // count), 0)
    return jnp.transpose(rows)


def picked(index_rows, table):
    count = index_rows.shape[0]
    columns = columns_of(index_rows)
    lanes = iota((128, table.shape[0]), 1)
    hot = [ones_where(columns[:, r : r + 1] == lanes) for r in range(count)]
    return dot(jnp.concatenate(hot, 0), table)


def normed_rows(values, gain):
    wide = values.astype(F32)
    mean = jnp.mean(wide * wide, axis=-1, keepdims=True)
    return (wide * lax.rsqrt(mean + 1e-06) * gain).astype(BF16)


def prepare(ids_ref, owner_ref, target_ref, nodes_ref, border_ref, request_ref, place_ref, *, dims):
    bricks, capacity = dims
    edges = owner_ref.shape[1]
    border_ref[...] = picked(ids_ref[...], nodes_ref[...]).astype(BF16)
    owner = owner_ref[...]
    target = target_ref[...]
    mine = iota((bricks, edges), 0) == owner
    mine_f = jnp.where(mine, 1.0, 0.0)
    before = ones_where(iota((edges, edges), 0) < iota((edges, edges), 1))
    counts = dot(mine_f.astype(BF16), before)
    slots = jnp.sum(counts * mine_f, axis=0, keepdims=True).astype(jnp.int32)
    place = owner * capacity + slots
    for r in range(edges // 128):
        place_ref[r : r + 1, :] = place[:, r * 128 : (r + 1) * 128]
    at_slot = ones_where(iota((128, edges), 0) == slots)
    high = (mine_f * (target >> 5).astype(F32)).astype(BF16)
    low = (mine_f * (target & 31).astype(F32)).astype(BF16)
    request = dot_nt(high, at_slot) * 32.0 + dot_nt(low, at_slot)
    request_ref[:bricks, :] = request.astype(jnp.int32)
    if request_ref.shape[0] > bricks:
        request_ref[bricks:, :] = jnp.zeros_like(request_ref[bricks:, :])


def project(nodes_ref, gain_ref, w_ref, q_ref, kv_ref):
    width = nodes_ref.shape[1]
    normed = normed_rows(nodes_ref[...], gain_ref[...])
    scale = 1.4426950408889634 / HEAD_DIM**0.5
    q_ref[...] = (dot(normed, w_ref[:, :width]) * scale).astype(BF16)
    kv_ref[...] = dot(normed, w_ref[:, width:]).astype(BF16)


def attend(*refs, pieces):
    valid_ref, nodes_ref, q_ref, kv_ref = refs[:4]
    halo_refs = refs[4 : 4 + pieces]
    (
        mask_ref,
        gain_ref,
        w_qkv_ref,
        w_out_ref,
        w_target_ref,
        request_ref,
        state_ref,
        answer_ref,
        v_ref,
    ) = refs[4 + pieces :]
    rows, width = q_ref.shape
    blocks = rows // BLOCK
    keys = v_ref.shape[1]
    border = halo_refs[0].shape[0]
    halo_nodes = jnp.concatenate([ref[...] for ref in halo_refs], 0)
    halo = dot(normed_rows(halo_nodes, gain_ref[...]), w_qkv_ref[:, width:]).astype(BF16)
    low_keys = iota((keys, PAIR), 1) < HEAD_DIM
    low = iota((rows, PAIR), 1) < HEAD_DIM

    lane = iota((blocks, 128), 1)
    row = iota((blocks, 128), 0)
    seen = dot(mask_ref[...].astype(F32).astype(BF16), ones_where(row == lane))
    seen = jnp.where(row == lane, 1.0, seen)
    for h in range(pieces):
        seen = jnp.where(lane == blocks + h, valid_ref[h].astype(F32), seen)
    bias = jnp.where(seen > 0.5, 0.0, -1e30).astype(BF16)
    bias = jnp.concatenate(
        [jnp.broadcast_to(bias[b : b + 1, :], (BLOCK, 128)) for b in range(blocks)], 0
    )
    own = iota((rows, 128), 0) // BLOCK
    far = blocks + iota((keys - rows, 128), 0) // border
    key_block = jnp.concatenate(
        [ones_where(own == iota(own.shape, 1)), ones_where(far == iota(far.shape, 1))], 0
    )

    attended = []
    for pair in range(width // PAIR):
        at = slice(pair * PAIR, (pair + 1) * PAIR)
        v_at = slice(width + pair * PAIR, width + (pair + 1) * PAIR)
        values = jnp.concatenate([kv_ref[:, v_at], halo[:, v_at]], 0)
        one = jnp.ones_like(values)
        v_ref[2 * pair] = jnp.where(low_keys, values, one)
        v_ref[2 * pair + 1] = jnp.where(low_keys, one, values)
        q_pair = q_ref[:, at]
        k_pair = jnp.concatenate([kv_ref[:, at], halo[:, at]], 0)
        k_pair = jnp.concatenate([k_pair, key_block], 1)
        mixed = []
        for half in range(2):
            q_own = jnp.where(low if half == 0 else ~low, q_pair, jnp.zeros_like(q_pair))
            scores = dot_nt(jnp.concatenate([q_own, bias], 1), k_pair)
            fold = scores[:, :128]
            for c in range(128, keys, 128):
                fold = jnp.maximum(fold, scores[:, c : c + 128])
            top = jnp.max(fold, axis=1, keepdims=True)
            weights = jnp.exp2((scores - top).astype(BF16))
            mixed.append(dot(weights, v_ref[2 * pair + half]))
        total = pltpu.roll(jnp.where(low, mixed[1], mixed[0]), HEAD_DIM, 1)
        attended.append((jnp.where(low, mixed[0], mixed[1]) / total).astype(BF16))
    state = nodes_ref[...].astype(F32) + dot(jnp.concatenate(attended, 1), w_out_ref[...])
    state = state.astype(BF16)
    state_ref[...] = state
    table = dot(state, w_target_ref[...]).astype(BF16)
    answer_ref[...] = picked(request_ref[...], table).astype(BF16)


def own_part(index_ref, state_ref, w_source_ref, contact_ref, w_ref, out_ref):
    rows = picked(index_ref[...], state_ref[...]).astype(BF16)
    rows = dot(rows, w_source_ref[...]).astype(BF16).astype(F32)
    out_ref[...] = rows + dot(contact_ref[...], w_ref[...])


def score(place_ref, answers_ref, part_ref, w_ref, out_ref):
    pre = part_ref[...] + picked(place_ref[...], answers_ref[...])
    weighted = jax.nn.gelu(pre) * w_ref[...]
    folded = weighted[:, :128]
    for at in range(128, weighted.shape[1], 128):
        folded = folded + weighted[:, at : at + 128]
    out_ref[...] = jnp.sum(jnp.transpose(folded), axis=0, keepdims=True)


def shape(dims, dtype):
    return jax.ShapeDtypeStruct(dims, dtype)


def neighbours(block):
    pieces, valid = [], []
    for axis in ("gy", "gz"):
        count = lax.axis_size(axis)
        index = lax.axis_index(axis)
        for first in range(min(2, count - 1)):
            swaps = []
            for i in range(first, count - 1, 2):
                swaps += [(i, i + 1), (i + 1, i)]
            pieces.append(lax.ppermute(block, axis, swaps))
            beside = jnp.where((index - first) % 2 == 0, index + 1, index - 1)
            valid.append((beside >= 0) & (beside < count))
    return pieces, jnp.stack(valid).astype(jnp.int32)


def local(
    nodes,
    block_mask,
    border_ids,
    contact,
    edge_source,
    edge_target,
    edge_owner,
    norm_gain,
    w_qkv,
    w_attn_out,
    w_source,
    w_target,
    w_contact,
    w_score,
):
    rows, width = nodes.shape
    edges = edge_source.shape[0]
    border_count = border_ids.shape[0]
    bricks = lax.axis_size("gy") * lax.axis_size("gz")
    capacity = max(2 * edges // bricks, 2)
    vmem = pltpu.CompilerParams(vmem_limit_bytes=60 * 1024 * 1024)

    border, request, place = pl.pallas_call(
        functools.partial(prepare, dims=(bricks, capacity)),
        out_shape=(
            shape((border_count, width), BF16),
            shape((max(256, bricks), 128), jnp.int32),
            shape((edges // 128, 128), jnp.int32),
        ),
        compiler_params=vmem,
    )(
        border_ids.reshape(border_count // 128, 128),
        edge_owner.reshape(1, edges),
        edge_target.reshape(1, edges),
        nodes,
    )
    halo, valid = neighbours(border)
    requests = lax.all_gather(request, ("gy", "gz"))
    me = lax.axis_index("gy") * lax.axis_size("gz") + lax.axis_index("gz")
    asked = lax.dynamic_index_in_dim(requests, me, 1, keepdims=False)[:, :capacity]
    asked = asked.reshape(bricks * capacity // 128, 128)

    gain = norm_gain.reshape(1, width)
    q, kv = pl.pallas_call(
        project,
        out_shape=(shape((rows, width), BF16), shape((rows, 2 * width), BF16)),
        grid=(rows // SPAN,),
        in_specs=[
            pl.BlockSpec((SPAN, width), lambda i: (i, 0)),
            pl.BlockSpec((1, width), lambda i: (0, 0)),
            pl.BlockSpec((width, 3 * width), lambda i: (0, 0)),
        ],
        out_specs=(
            pl.BlockSpec((SPAN, width), lambda i: (i, 0)),
            pl.BlockSpec((SPAN, 2 * width), lambda i: (i, 0)),
        ),
        compiler_params=vmem,
    )(nodes, gain, w_qkv)

    keys = rows + len(halo) * border_count
    in_vmem = pl.BlockSpec(memory_space=pltpu.VMEM)
    node_state, answers = pl.pallas_call(
        functools.partial(attend, pieces=len(halo)),
        out_shape=(
            shape((rows, width), BF16),
            shape((bricks * capacity, w_target.shape[1]), BF16),
        ),
        in_specs=[pl.BlockSpec(memory_space=pltpu.SMEM)] + [in_vmem] * (9 + len(halo)),
        out_specs=(in_vmem, in_vmem),
        scratch_shapes=[pltpu.VMEM((HEADS, keys, PAIR), BF16)],
        compiler_params=vmem,
    )(valid, nodes, q, kv, *halo, block_mask, gain, w_qkv, w_attn_out, w_target, asked)

    hidden = w_target.shape[1]
    answers = lax.all_to_all(
        answers.reshape(bricks, capacity, hidden),
        ("gy", "gz"),
        split_axis=0,
        concat_axis=0,
        tiled=True,
    ).reshape(bricks * capacity, hidden)
    part = pl.pallas_call(
        own_part, out_shape=shape((edges, hidden), F32), compiler_params=vmem
    )(edge_source.reshape(edges // 128, 128), node_state, w_source, contact, w_contact)
    scores = pl.pallas_call(score, out_shape=shape((1, edges), F32), compiler_params=vmem)(
        place, answers, part, w_score.reshape(1, hidden)
    )
    return (node_state, scores.reshape(edges))


def solution(mesh):
    split = ("groups", "gy", "gz")
    in_specs = (
        P(split, None),
        P(split, None),
        P(split),
        P(split, None),
        P(split),
        P(split),
        P(split, None),
        P(),
        P(),
        P(),
        P(),
        P(),
        P(),
        P(),
    )
    out_specs = (P(split, None), P(split))
    return jax.shard_map(local, mesh=mesh, in_specs=in_specs, out_specs=out_specs, check_vma=False)
```

```python
import functools

import jax
import jax.numpy as jnp
from jax import lax
from jax.experimental import pallas as pl
from jax.experimental.pallas import tpu as pltpu
from jax.sharding import PartitionSpec as P

HEADS = 8
HEAD_DIM = 64
BLOCK = 128
PAIR = 2 * HEAD_DIM
SPAN = 256
F32 = jnp.float32
BF16 = jnp.bfloat16
NT = (((1,), (1,)), ((), ()))


def dot(lhs, rhs):
    return jnp.dot(lhs, rhs, preferred_element_type=F32)


def dot_nt(lhs, rhs):
    return lax.dot_general(lhs, rhs, NT, preferred_element_type=F32)


def ones_where(condition):
    return jnp.where(condition, 1.0, 0.0).astype(BF16)


def iota(shape, axis):
    return lax.broadcasted_iota(jnp.int32, shape, axis)


def columns_of(rows):
    count, lanes = rows.shape
    if count < 8:
        rows = jnp.concatenate([rows] * (8 // count), 0)
    return jnp.transpose(rows)


def picked(index_rows, table):
    count = index_rows.shape[0]
    columns = columns_of(index_rows)
    lanes = iota((128, table.shape[0]), 1)
    hot = [ones_where(columns[:, r : r + 1] == lanes) for r in range(count)]
    return dot(jnp.concatenate(hot, 0), table)


def normed_rows(values, gain):
    wide = values.astype(F32)
    mean = jnp.mean(wide * wide, axis=-1, keepdims=True)
    return (wide * lax.rsqrt(mean + 1e-06) * gain).astype(BF16)


def prepare(ids_ref, owner_ref, target_ref, nodes_ref, border_ref, request_ref, place_ref, *, dims):
    bricks, capacity = dims
    edges = owner_ref.shape[1]
    border = ids_ref.shape[0] * 128
    border_ref[:border, :] = picked(ids_ref[...], nodes_ref[...]).astype(BF16)
    border_ref[border:, :] = jnp.ones_like(border_ref[border:, :])
    owner = owner_ref[...]
    target = target_ref[...]
    mine = iota((bricks, edges), 0) == owner
    mine_f = jnp.where(mine, 1.0, 0.0)
    before = ones_where(iota((edges, edges), 0) < iota((edges, edges), 1))
    counts = dot(mine_f.astype(BF16), before)
    slots = jnp.sum(counts * mine_f, axis=0, keepdims=True).astype(jnp.int32)
    place = owner * capacity + slots
    for r in range(edges // 128):
        place_ref[r : r + 1, :] = place[:, r * 128 : (r + 1) * 128]
    at_slot = ones_where(iota((128, edges), 0) == slots)
    high = (mine_f * (target >> 5).astype(F32)).astype(BF16)
    low = (mine_f * (target & 31).astype(F32)).astype(BF16)
    request = dot_nt(high, at_slot) * 32.0 + dot_nt(low, at_slot)
    request_ref[...] = request.astype(jnp.int32)


def project(nodes_ref, gain_ref, w_ref, q_ref, kv_ref):
    width = nodes_ref.shape[1]
    normed = normed_rows(nodes_ref[...], gain_ref[...])
    scale = 1.4426950408889634 / HEAD_DIM**0.5
    q_ref[...] = (dot(normed, w_ref[:, :width]) * scale).astype(BF16)
    kv_ref[...] = dot(normed, w_ref[:, width:]).astype(BF16)


def attend(*refs, pieces):
    nodes_ref, q_ref, kv_ref = refs[:3]
    halo_refs = refs[3 : 3 + pieces]
    (
        mask_ref,
        gain_ref,
        w_qkv_ref,
        w_out_ref,
        w_target_ref,
        request_ref,
        state_ref,
        answer_ref,
        v_ref,
    ) = refs[3 + pieces :]
    rows, width = q_ref.shape
    blocks = rows // BLOCK
    keys = v_ref.shape[1]
    border = (keys - rows) // pieces
    halo_nodes = jnp.concatenate([ref[:border, :] for ref in halo_refs], 0)
    halo = dot(normed_rows(halo_nodes, gain_ref[...]), w_qkv_ref[:, width:]).astype(BF16)
    low_keys = iota((keys, PAIR), 1) < HEAD_DIM
    low = iota((rows, PAIR), 1) < HEAD_DIM

    lane = iota((blocks, 128), 1)
    row = iota((blocks, 128), 0)
    seen = dot(mask_ref[...].astype(F32).astype(BF16), ones_where(row == lane))
    seen = jnp.where(row == lane, 1.0, seen)
    for h in range(pieces):
        sent = halo_refs[h][border : border + 1, :128].astype(F32)
        seen = jnp.where(lane == blocks + h, sent, seen)
    bias = jnp.where(seen > 0.5, 0.0, -1e30).astype(BF16)
    bias = jnp.concatenate(
        [jnp.broadcast_to(bias[b : b + 1, :], (BLOCK, 128)) for b in range(blocks)], 0
    )
    own = iota((rows, 128), 0) // BLOCK
    far = blocks + iota((keys - rows, 128), 0) // border
    key_block = jnp.concatenate(
        [ones_where(own == iota(own.shape, 1)), ones_where(far == iota(far.shape, 1))], 0
    )

    attended = []
    for pair in range(width // PAIR):
        at = slice(pair * PAIR, (pair + 1) * PAIR)
        v_at = slice(width + pair * PAIR, width + (pair + 1) * PAIR)
        values = jnp.concatenate([kv_ref[:, v_at], halo[:, v_at]], 0)
        one = jnp.ones_like(values)
        v_ref[2 * pair] = jnp.where(low_keys, values, one)
        v_ref[2 * pair + 1] = jnp.where(low_keys, one, values)
        q_pair = q_ref[:, at]
        k_pair = jnp.concatenate([kv_ref[:, at], halo[:, at]], 0)
        k_pair = jnp.concatenate([k_pair, key_block], 1)
        mixed = []
        for half in range(2):
            q_own = jnp.where(low if half == 0 else ~low, q_pair, jnp.zeros_like(q_pair))
            scores = dot_nt(jnp.concatenate([q_own, bias], 1), k_pair)
            fold = scores[:, :128]
            for c in range(128, keys, 128):
                fold = jnp.maximum(fold, scores[:, c : c + 128])
            top = jnp.max(fold, axis=1, keepdims=True)
            weights = jnp.exp2((scores - top).astype(BF16))
            mixed.append(dot(weights, v_ref[2 * pair + half]))
        total = pltpu.roll(jnp.where(low, mixed[1], mixed[0]), HEAD_DIM, 1)
        attended.append((jnp.where(low, mixed[0], mixed[1]) / total).astype(BF16))
    state = nodes_ref[...].astype(F32) + dot(jnp.concatenate(attended, 1), w_out_ref[...])
    state = state.astype(BF16)
    state_ref[...] = state
    table = dot(state, w_target_ref[...]).astype(BF16)
    bricks = request_ref.shape[0]
    capacity = answer_ref.shape[0] // bricks
    columns = jnp.transpose(request_ref[...])
    lanes = iota((capacity, rows), 1)
    hot = [ones_where(columns[:capacity, b : b + 1] == lanes) for b in range(bricks)]
    answer_ref[...] = dot(jnp.concatenate(hot, 0), table).astype(BF16)


def own_part(index_ref, state_ref, w_source_ref, contact_ref, w_ref, out_ref):
    rows = picked(index_ref[...], state_ref[...]).astype(BF16)
    rows = dot(rows, w_source_ref[...]).astype(BF16).astype(F32)
    out_ref[...] = rows + dot(contact_ref[...], w_ref[...])


def score(place_ref, answers_ref, part_ref, w_ref, out_ref):
    pre = part_ref[...] + picked(place_ref[...], answers_ref[...])
    weighted = jax.nn.gelu(pre) * w_ref[...]
    folded = weighted[:, :128]
    for at in range(128, weighted.shape[1], 128):
        folded = folded + weighted[:, at : at + 128]
    out_ref[...] = jnp.sum(jnp.transpose(folded), axis=0, keepdims=True)


def shape(dims, dtype):
    return jax.ShapeDtypeStruct(dims, dtype)


def neighbours(block):
    pieces = []
    for axis in ("gy", "gz"):
        count = lax.axis_size(axis)
        for first in range(min(2, count - 1)):
            swaps = []
            for i in range(first, count - 1, 2):
                swaps += [(i, i + 1), (i + 1, i)]
            pieces.append(lax.ppermute(block, axis, swaps))
    return pieces


def local(
    nodes,
    block_mask,
    border_ids,
    contact,
    edge_source,
    edge_target,
    edge_owner,
    norm_gain,
    w_qkv,
    w_attn_out,
    w_source,
    w_target,
    w_contact,
    w_score,
):
    rows, width = nodes.shape
    edges = edge_source.shape[0]
    border_count = border_ids.shape[0]
    bricks = lax.axis_size("gy") * lax.axis_size("gz")
    capacity = max(2 * edges // bricks, 2)
    vmem = pltpu.CompilerParams(vmem_limit_bytes=60 * 1024 * 1024)

    border, request, place = pl.pallas_call(
        functools.partial(prepare, dims=(bricks, capacity)),
        out_shape=(
            shape((border_count + 16, width), BF16),
            shape((bricks, 128), jnp.int32),
            shape((edges // 128, 128), jnp.int32),
        ),
        compiler_params=vmem,
    )(
        border_ids.reshape(border_count // 128, 128),
        edge_owner.reshape(1, edges),
        edge_target.reshape(1, edges),
        nodes,
    )
    asked = lax.all_to_all(request, ("gy", "gz"), split_axis=0, concat_axis=0, tiled=True)
    halo = neighbours(border)

    gain = norm_gain.reshape(1, width)
    q, kv = pl.pallas_call(
        project,
        out_shape=(shape((rows, width), BF16), shape((rows, 2 * width), BF16)),
        grid=(rows // SPAN,),
        in_specs=[
            pl.BlockSpec((SPAN, width), lambda i: (i, 0)),
            pl.BlockSpec((1, width), lambda i: (0, 0)),
            pl.BlockSpec((width, 3 * width), lambda i: (0, 0)),
        ],
        out_specs=(
            pl.BlockSpec((SPAN, width), lambda i: (i, 0)),
            pl.BlockSpec((SPAN, 2 * width), lambda i: (i, 0)),
        ),
        compiler_params=vmem,
    )(nodes, gain, w_qkv)

    keys = rows + len(halo) * border_count
    in_vmem = pl.BlockSpec(memory_space=pltpu.VMEM)
    node_state, answers = pl.pallas_call(
        functools.partial(attend, pieces=len(halo)),
        out_shape=(
            shape((rows, width), BF16),
            shape((bricks * capacity, w_target.shape[1]), BF16),
        ),
        in_specs=[in_vmem] * (9 + len(halo)),
        out_specs=(in_vmem, in_vmem),
        scratch_shapes=[pltpu.VMEM((HEADS, keys, PAIR), BF16)],
        compiler_params=vmem,
    )(nodes, q, kv, *halo, block_mask, gain, w_qkv, w_attn_out, w_target, asked)

    hidden = w_target.shape[1]
    answers = lax.all_to_all(
        answers.reshape(bricks, capacity, hidden),
        ("gy", "gz"),
        split_axis=0,
        concat_axis=0,
        tiled=True,
    ).reshape(bricks * capacity, hidden)
    part = pl.pallas_call(
        own_part, out_shape=shape((edges, hidden), F32), compiler_params=vmem
    )(edge_source.reshape(edges // 128, 128), node_state, w_source, contact, w_contact)
    scores = pl.pallas_call(score, out_shape=shape((1, edges), F32), compiler_params=vmem)(
        place, answers, part, w_score.reshape(1, hidden)
    )
    return (node_state, scores.reshape(edges))


def solution(mesh):
    split = ("groups", "gy", "gz")
    in_specs = (
        P(split, None),
        P(split, None),
        P(split),
        P(split, None),
        P(split),
        P(split),
        P(split, None),
        P(),
        P(),
        P(),
        P(),
        P(),
        P(),
        P(),
    )
    out_specs = (P(split, None), P(split))
    return jax.shard_map(local, mesh=mesh, in_specs=in_specs, out_specs=out_specs, check_vma=False)
```

```python
import functools

import jax
import jax.numpy as jnp
from jax import lax
from jax.experimental import pallas as pl
from jax.experimental.pallas import tpu as pltpu
from jax.sharding import PartitionSpec as P

HEADS = 8
HEAD_DIM = 64
BLOCK = 128
PAIR = 2 * HEAD_DIM
F32 = jnp.float32
BF16 = jnp.bfloat16
NT = (((1,), (1,)), ((), ()))


def dot(lhs, rhs):
    return jnp.dot(lhs, rhs, preferred_element_type=F32)


def dot_nt(lhs, rhs):
    return lax.dot_general(lhs, rhs, NT, preferred_element_type=F32)


def ones_where(condition):
    return jnp.where(condition, 1.0, 0.0).astype(BF16)


def iota(shape, axis):
    return lax.broadcasted_iota(jnp.int32, shape, axis)


def columns_of(rows):
    count, lanes = rows.shape
    if count < 8:
        rows = jnp.concatenate([rows] * (8 // count), 0)
    return jnp.transpose(rows)


def hot_rows(index_rows, size):
    count = index_rows.shape[0]
    columns = columns_of(index_rows)
    lanes = iota((128, size), 1)
    return jnp.concatenate([ones_where(columns[:, r : r + 1] == lanes) for r in range(count)], 0)


def picked(index_rows, table):
    return dot(hot_rows(index_rows, table.shape[0]), table)


def normed_rows(values, gain):
    wide = values.astype(F32)
    mean = jnp.mean(wide * wide, axis=-1, keepdims=True)
    return (wide * lax.rsqrt(mean + 1e-06) * gain).astype(BF16)


def prepare(ids_ref, owner_ref, target_ref, nodes_ref, border_ref, request_ref, place_ref, *, dims):
    bricks, capacity = dims
    edges = owner_ref.shape[1]
    border = ids_ref.shape[0] * 128
    border_ref[:border, :] = picked(ids_ref[...], nodes_ref[...]).astype(BF16)
    border_ref[border:, :] = jnp.ones_like(border_ref[border:, :])
    owner = owner_ref[...]
    target = target_ref[...]
    mine = iota((bricks, edges), 0) == owner
    mine_f = jnp.where(mine, 1.0, 0.0)
    before = ones_where(iota((edges, edges), 0) < iota((edges, edges), 1))
    counts = dot(mine_f.astype(BF16), before)
    slots = jnp.sum(counts * mine_f, axis=0, keepdims=True).astype(jnp.int32)
    place = owner * capacity + slots
    for r in range(edges // 128):
        place_ref[r : r + 1, :] = place[:, r * 128 : (r + 1) * 128]
    at_slot = ones_where(iota((128, edges), 0) == slots)
    high = (mine_f * (target >> 5).astype(F32)).astype(BF16)
    low = (mine_f * (target & 31).astype(F32)).astype(BF16)
    request = dot_nt(high, at_slot) * 32.0 + dot_nt(low, at_slot)
    request_ref[...] = request.astype(jnp.int32)


def project(nodes_ref, gain_ref, w_ref, request_ref, q_ref, kv_ref, column_ref):
    width = nodes_ref.shape[1]
    normed = normed_rows(nodes_ref[...], gain_ref[...])
    scale = 1.4426950408889634 / HEAD_DIM**0.5
    q_ref[...] = (dot(normed, w_ref[:, :width]) * scale).astype(BF16)
    kv_ref[...] = dot(normed, w_ref[:, width:]).astype(BF16)
    column_ref[...] = jnp.transpose(request_ref[...])


def attend(*refs, pieces):
    nodes_ref, q_ref, kv_ref = refs[:3]
    halo_refs = refs[3 : 3 + pieces]
    (
        mask_ref,
        gain_ref,
        w_qkv_ref,
        w_out_ref,
        w_target_ref,
        column_ref,
        state_ref,
        answer_ref,
        v_ref,
    ) = refs[3 + pieces :]
    rows, width = q_ref.shape
    blocks = rows // BLOCK
    keys = v_ref.shape[1]
    border = (keys - rows) // pieces
    halo_nodes = jnp.concatenate([ref[:border, :] for ref in halo_refs], 0)
    halo = dot(normed_rows(halo_nodes, gain_ref[...]), w_qkv_ref[:, width:]).astype(BF16)
    low_keys = iota((keys, PAIR), 1) < HEAD_DIM
    low = iota((rows, PAIR), 1) < HEAD_DIM

    lane = iota((blocks, 128), 1)
    row = iota((blocks, 128), 0)
    seen = dot(mask_ref[...].astype(F32).astype(BF16), ones_where(row == lane))
    seen = jnp.where(row == lane, 1.0, seen)
    for h in range(pieces):
        sent = halo_refs[h][border : border + 1, :128].astype(F32)
        seen = jnp.where(lane == blocks + h, sent, seen)
    bias = jnp.where(seen > 0.5, 0.0, -1e30).astype(BF16)
    bias = jnp.concatenate(
        [jnp.broadcast_to(bias[b : b + 1, :], (BLOCK, 128)) for b in range(blocks)], 0
    )
    own = iota((rows, 128), 0) // BLOCK
    far = blocks + iota((keys - rows, 128), 0) // border
    key_block = jnp.concatenate(
        [ones_where(own == iota(own.shape, 1)), ones_where(far == iota(far.shape, 1))], 0
    )

    attended = []
    for pair in range(width // PAIR):
        at = slice(pair * PAIR, (pair + 1) * PAIR)
        v_at = slice(width + pair * PAIR, width + (pair + 1) * PAIR)
        values = jnp.concatenate([kv_ref[:, v_at], halo[:, v_at]], 0)
        one = jnp.ones_like(values)
        v_ref[2 * pair] = jnp.where(low_keys, values, one)
        v_ref[2 * pair + 1] = jnp.where(low_keys, one, values)
        q_pair = q_ref[:, at]
        k_pair = jnp.concatenate([kv_ref[:, at], halo[:, at]], 0)
        k_pair = jnp.concatenate([k_pair, key_block], 1)
        mixed = []
        for half in range(2):
            q_own = jnp.where(low if half == 0 else ~low, q_pair, jnp.zeros_like(q_pair))
            scores = dot_nt(jnp.concatenate([q_own, bias], 1), k_pair)
            fold = scores[:, :128]
            for c in range(128, keys, 128):
                fold = jnp.maximum(fold, scores[:, c : c + 128])
            top = jnp.max(fold, axis=1, keepdims=True)
            weights = jnp.exp2((scores - top).astype(BF16))
            mixed.append(dot(weights, v_ref[2 * pair + half]))
        total = pltpu.roll(jnp.where(low, mixed[1], mixed[0]), HEAD_DIM, 1)
        attended.append((jnp.where(low, mixed[0], mixed[1]) / total).astype(BF16))
    state = nodes_ref[...].astype(F32) + dot(jnp.concatenate(attended, 1), w_out_ref[...])
    state = state.astype(BF16)
    state_ref[...] = state
    table = dot(state, w_target_ref[...]).astype(BF16)
    bricks = column_ref.shape[1]
    capacity = answer_ref.shape[0] // bricks
    columns = column_ref[...]
    lanes = iota((capacity, rows), 1)
    hot = [ones_where(columns[:capacity, b : b + 1] == lanes) for b in range(bricks)]
    answer_ref[...] = dot(jnp.concatenate(hot, 0), table).astype(BF16)


def own_part(
    index_ref, state_ref, w_source_ref, contact_ref, w_ref, part_ref
):
    rows = picked(index_ref[...], state_ref[...]).astype(BF16)
    rows = dot(rows, w_source_ref[...]).astype(BF16).astype(F32)
    part_ref[...] = rows + dot(contact_ref[...], w_ref[...])


def score(place_ref, answers_ref, part_ref, w_ref, out_ref):
    pre = part_ref[...] + picked(place_ref[...], answers_ref[...])
    weighted = jax.nn.gelu(pre) * w_ref[...]
    folded = weighted[:, :128]
    for at in range(128, weighted.shape[1], 128):
        folded = folded + weighted[:, at : at + 128]
    out_ref[...] = jnp.sum(jnp.transpose(folded), axis=0, keepdims=True)


def near(array):
    return pltpu.with_memory_space_constraint(array, pltpu.VMEM)


def run(kernel, outs, *args, scratch=(), mib=16):
    space = pl.BlockSpec(memory_space=pltpu.VMEM)
    return pl.pallas_call(
        kernel,
        out_shape=tuple(outs),
        in_specs=[space] * len(args),
        out_specs=(space,) * len(outs),
        scratch_shapes=scratch,
        compiler_params=pltpu.CompilerParams(vmem_limit_bytes=mib * 1024 * 1024),
    )(*args)


def shape(dims, dtype):
    return jax.ShapeDtypeStruct(dims, dtype)


def neighbours(block):
    pieces = []
    for axis in ("gy", "gz"):
        count = lax.axis_size(axis)
        for first in range(min(2, count - 1)):
            swaps = []
            for i in range(first, count - 1, 2):
                swaps += [(i, i + 1), (i + 1, i)]
            pieces.append(lax.ppermute(block, axis, swaps))
    return pieces


def local(
    nodes,
    block_mask,
    border_ids,
    contact,
    edge_source,
    edge_target,
    edge_owner,
    norm_gain,
    w_qkv,
    w_attn_out,
    w_source,
    w_target,
    w_contact,
    w_score,
):
    rows, width = nodes.shape
    edges = edge_source.shape[0]
    border_count = border_ids.shape[0]
    bricks = lax.axis_size("gy") * lax.axis_size("gz")
    capacity = max(2 * edges // bricks, 2)
    hidden = w_target.shape[1]
    nodes_near = near(nodes)
    border, request, place = run(
        functools.partial(prepare, dims=(bricks, capacity)),
        (
            shape((border_count + 16, width), BF16),
            shape((bricks, 128), jnp.int32),
            shape((edges // 128, 128), jnp.int32),
        ),
        border_ids.reshape(border_count // 128, 128),
        edge_owner.reshape(1, edges),
        edge_target.reshape(1, edges),
        nodes_near,
    )
    halo = neighbours(border)
    asked = lax.all_to_all(request, ("gy", "gz"), split_axis=0, concat_axis=0, tiled=True)

    gain = norm_gain.reshape(1, width)
    w_qkv_near = near(w_qkv)
    q, kv, columns = run(
        project,
        (
            pltpu.VMEM((rows, width), BF16),
            pltpu.VMEM((rows, 2 * width), BF16),
            pltpu.VMEM((128, bricks), jnp.int32),
        ),
        nodes_near,
        gain,
        w_qkv_near,
        near(asked),
    )
    node_state, answers = run(
        functools.partial(attend, pieces=len(halo)),
        (shape((rows, width), BF16), shape((bricks * capacity, hidden), BF16)),
        nodes_near,
        q,
        kv,
        *[near(piece) for piece in halo],
        block_mask,
        gain,
        w_qkv_near,
        near(w_attn_out),
        near(w_target),
        columns,
        mib=32,
        scratch=[pltpu.VMEM((HEADS, rows + len(halo) * border_count, PAIR), BF16)],
    )
    answers = lax.all_to_all(
        answers.reshape(bricks, capacity, hidden),
        ("gy", "gz"),
        split_axis=0,
        concat_axis=0,
        tiled=True,
    ).reshape(bricks * capacity, hidden)
    (part,) = run(
        own_part,
        (shape((edges, hidden), F32),),
        edge_source.reshape(edges // 128, 128),
        node_state,
        w_source,
        contact,
        w_contact,
    )
    (scores,) = run(
        score, (shape((1, edges), F32),), place, near(answers), part, w_score.reshape(1, hidden)
    )
    return (node_state, scores.reshape(edges))


def solution(mesh):
    split = ("groups", "gy", "gz")
    in_specs = (
        P(split, None),
        P(split, None),
        P(split),
        P(split, None),
        P(split),
        P(split),
        P(split, None),
        P(),
        P(),
        P(),
        P(),
        P(),
        P(),
        P(),
    )
    out_specs = (P(split, None), P(split))
    return jax.shard_map(local, mesh=mesh, in_specs=in_specs, out_specs=out_specs, check_vma=False)
```

```python
import functools

import jax
import jax.numpy as jnp
from jax import lax
from jax.experimental import pallas as pl
from jax.experimental.pallas import tpu as pltpu
from jax.sharding import PartitionSpec as P

HEADS = 8
HEAD_DIM = 64
BLOCK = 128
PAIR = 2 * HEAD_DIM
F32 = jnp.float32
BF16 = jnp.bfloat16
FAR = pltpu.HBM
NT = (((1,), (1,)), ((), ()))


def dot(lhs, rhs):
    return jnp.dot(lhs, rhs, preferred_element_type=F32)


def dot_nt(lhs, rhs):
    return lax.dot_general(lhs, rhs, NT, preferred_element_type=F32)


def ones_where(condition):
    return jnp.where(condition, 1.0, 0.0).astype(BF16)


def iota(shape, axis):
    return lax.broadcasted_iota(jnp.int32, shape, axis)


def columns_of(rows):
    count, lanes = rows.shape
    if count < 8:
        rows = jnp.concatenate([rows] * (8 // count), 0)
    return jnp.transpose(rows)


def hot_rows(index_rows, size):
    count = index_rows.shape[0]
    columns = columns_of(index_rows)
    lanes = iota((128, size), 1)
    return jnp.concatenate([ones_where(columns[:, r : r + 1] == lanes) for r in range(count)], 0)


def picked(index_rows, table):
    return dot(hot_rows(index_rows, table.shape[0]), table)


def normed_rows(values, gain):
    wide = values.astype(F32)
    mean = jnp.mean(wide * wide, axis=-1, keepdims=True)
    return (wide * lax.rsqrt(mean + 1e-06) * gain).astype(BF16)


def fetch(sources, places, signals):
    copies = [
        pltpu.make_async_copy(source, place, signals.at[i])
        for i, (source, place) in enumerate(zip(sources, places))
    ]
    for copy in copies:
        copy.start()
    return copies


def prepare(*refs, dims):
    border_ref, request_ref, place_ref, ids_ref, owner_ref, target_ref, nodes_ref, signals = refs[4:]
    copies = fetch(refs[:4], (ids_ref, owner_ref, target_ref, nodes_ref), signals)
    for copy in copies[:3]:
        copy.wait()
    bricks, capacity = dims
    edges = owner_ref.shape[1]
    owner = owner_ref[...]
    target = target_ref[...]
    mine = iota((bricks, edges), 0) == owner
    mine_f = jnp.where(mine, 1.0, 0.0)
    before = ones_where(iota((edges, edges), 0) < iota((edges, edges), 1))
    counts = dot(mine_f.astype(BF16), before)
    slots = jnp.sum(counts * mine_f, axis=0, keepdims=True).astype(jnp.int32)
    place = owner * capacity + slots
    for r in range(edges // 128):
        place_ref[r : r + 1, :] = place[:, r * 128 : (r + 1) * 128]
    at_slot = ones_where(iota((128, edges), 0) == slots)
    high = (mine_f * (target >> 5).astype(F32)).astype(BF16)
    low = (mine_f * (target & 31).astype(F32)).astype(BF16)
    request = dot_nt(high, at_slot) * 32.0 + dot_nt(low, at_slot)
    request_ref[...] = request.astype(jnp.int32)
    border = ids_ref.shape[0] * 128
    hot = hot_rows(ids_ref[...], nodes_ref.shape[0])
    copies[3].wait()
    border_ref[:border, :] = dot(hot, nodes_ref[...]).astype(BF16)
    border_ref[border:, :] = jnp.ones_like(border_ref[border:, :])


def project(*refs):
    q_ref, kv_ref, nodes_ref, gain_ref, w_ref, signals = refs[3:]
    copies = fetch(refs[:3], (nodes_ref, gain_ref, w_ref), signals)
    width = nodes_ref.shape[1]
    copies[0].wait()
    copies[1].wait()
    normed = normed_rows(nodes_ref[...], gain_ref[...])
    scale = 1.4426950408889634 / HEAD_DIM**0.5
    copies[2].wait()
    q_ref[...] = (dot(normed, w_ref[:, :width]) * scale).astype(BF16)
    kv_ref[...] = dot(normed, w_ref[:, width:]).astype(BF16)


def attend(*refs, pieces):
    far_refs = refs[:6]
    q_ref, kv_ref, request_ref = refs[6:9]
    halo_refs = refs[9 : 9 + pieces]
    state_ref, answer_ref, v_ref = refs[9 + pieces : 12 + pieces]
    mask_ref, gain_ref, w_kv_ref, nodes_ref, w_out_ref, w_target_ref, signals = refs[12 + pieces :]
    rows, width = q_ref.shape
    sources = list(far_refs)
    sources[2] = far_refs[2].at[:, width:]
    copies = fetch(
        sources, (mask_ref, gain_ref, w_kv_ref, nodes_ref, w_out_ref, w_target_ref), signals
    )
    for copy in copies[:3]:
        copy.wait()
    blocks = rows // BLOCK
    keys = v_ref.shape[1]
    border = (keys - rows) // pieces
    halo_nodes = jnp.concatenate([ref[:border, :] for ref in halo_refs], 0)
    halo = dot(normed_rows(halo_nodes, gain_ref[...]), w_kv_ref[...]).astype(BF16)
    low_keys = iota((keys, PAIR), 1) < HEAD_DIM
    low = iota((rows, PAIR), 1) < HEAD_DIM

    lane = iota((blocks, 128), 1)
    row = iota((blocks, 128), 0)
    seen = dot(mask_ref[...].astype(F32).astype(BF16), ones_where(row == lane))
    seen = jnp.where(row == lane, 1.0, seen)
    for h in range(pieces):
        sent = halo_refs[h][border : border + 1, :128].astype(F32)
        seen = jnp.where(lane == blocks + h, sent, seen)
    bias = jnp.where(seen > 0.5, 0.0, -1e30).astype(BF16)
    bias = jnp.concatenate(
        [jnp.broadcast_to(bias[b : b + 1, :], (BLOCK, 128)) for b in range(blocks)], 0
    )
    own = iota((rows, 128), 0) // BLOCK
    far = blocks + iota((keys - rows, 128), 0) // border
    key_block = jnp.concatenate(
        [ones_where(own == iota(own.shape, 1)), ones_where(far == iota(far.shape, 1))], 0
    )

    attended = []
    for pair in range(width // PAIR):
        at = slice(pair * PAIR, (pair + 1) * PAIR)
        v_at = slice(width + pair * PAIR, width + (pair + 1) * PAIR)
        values = jnp.concatenate([kv_ref[:, v_at], halo[:, v_at]], 0)
        one = jnp.ones_like(values)
        v_ref[2 * pair] = jnp.where(low_keys, values, one)
        v_ref[2 * pair + 1] = jnp.where(low_keys, one, values)
        q_pair = q_ref[:, at]
        k_pair = jnp.concatenate([kv_ref[:, at], halo[:, at]], 0)
        k_pair = jnp.concatenate([k_pair, key_block], 1)
        mixed = []
        for half in range(2):
            q_own = jnp.where(low if half == 0 else ~low, q_pair, jnp.zeros_like(q_pair))
            scores = dot_nt(jnp.concatenate([q_own, bias], 1), k_pair)
            fold = scores[:, :128]
            for c in range(128, keys, 128):
                fold = jnp.maximum(fold, scores[:, c : c + 128])
            top = jnp.max(fold, axis=1, keepdims=True)
            weights = jnp.exp2((scores - top).astype(BF16))
            mixed.append(dot(weights, v_ref[2 * pair + half]))
        total = pltpu.roll(jnp.where(low, mixed[1], mixed[0]), HEAD_DIM, 1)
        attended.append((jnp.where(low, mixed[0], mixed[1]) / total).astype(BF16))
    for copy in copies[3:]:
        copy.wait()
    state = nodes_ref[...].astype(F32) + dot(jnp.concatenate(attended, 1), w_out_ref[...])
    state = state.astype(BF16)
    state_ref[...] = state
    table = dot(state, w_target_ref[...]).astype(BF16)
    bricks = request_ref.shape[0]
    capacity = answer_ref.shape[0] // bricks
    columns = jnp.transpose(request_ref[...])
    lanes = iota((capacity, rows), 1)
    hot = [ones_where(columns[:capacity, b : b + 1] == lanes) for b in range(bricks)]
    answer_ref[...] = dot(jnp.concatenate(hot, 0), table).astype(BF16)


def own_part(
    index_ref, state_ref, w_source_ref, contact_ref, w_ref, part_ref
):
    rows = picked(index_ref[...], state_ref[...]).astype(BF16)
    rows = dot(rows, w_source_ref[...]).astype(BF16).astype(F32)
    part_ref[...] = rows + dot(contact_ref[...], w_ref[...])


def score(place_ref, answers_ref, part_ref, w_ref, out_ref):
    pre = part_ref[...] + picked(place_ref[...], answers_ref[...])
    weighted = jax.nn.gelu(pre) * w_ref[...]
    folded = weighted[:, :128]
    for at in range(128, weighted.shape[1], 128):
        folded = folded + weighted[:, at : at + 128]
    out_ref[...] = jnp.sum(jnp.transpose(folded), axis=0, keepdims=True)


def near(array):
    return pltpu.with_memory_space_constraint(array, pltpu.VMEM)


def away(array):
    return pltpu.with_memory_space_constraint(array, pltpu.HBM)


def run(kernel, outs, *args, scratch=(), mib=16, far=0):
    space = pl.BlockSpec(memory_space=pltpu.VMEM)
    left = pl.BlockSpec(memory_space=FAR)
    args = [away(arg) for arg in args[:far]] + list(args[far:])
    return pl.pallas_call(
        kernel,
        out_shape=tuple(outs),
        in_specs=[left] * far + [space] * (len(args) - far),
        out_specs=(space,) * len(outs),
        scratch_shapes=scratch,
        compiler_params=pltpu.CompilerParams(vmem_limit_bytes=mib * 1024 * 1024),
    )(*args)


def shape(dims, dtype):
    return jax.ShapeDtypeStruct(dims, dtype)


def neighbours(block):
    steps = []
    for axis in ("gy", "gz"):
        count = lax.axis_size(axis)
        for first in range(min(2, count - 1)):
            swaps = []
            for i in range(first, count - 1, 2):
                swaps += [(i, i + 1), (i + 1, i)]
            steps.append((axis, swaps))
    return [lax.ppermute(block, axis, swaps) for axis, swaps in reversed(steps)]


def local(
    nodes,
    block_mask,
    border_ids,
    contact,
    edge_source,
    edge_target,
    edge_owner,
    norm_gain,
    w_qkv,
    w_attn_out,
    w_source,
    w_target,
    w_contact,
    w_score,
):
    rows, width = nodes.shape
    edges = edge_source.shape[0]
    border_count = border_ids.shape[0]
    bricks = lax.axis_size("gy") * lax.axis_size("gz")
    capacity = max(2 * edges // bricks, 2)
    hidden = w_target.shape[1]
    integer = jnp.int32
    border, request, place = run(
        functools.partial(prepare, dims=(bricks, capacity)),
        (
            shape((border_count + 16, width), BF16),
            shape((bricks, 128), integer),
            shape((edges // 128, 128), integer),
        ),
        border_ids.reshape(border_count // 128, 128),
        edge_owner.reshape(1, edges),
        edge_target.reshape(1, edges),
        nodes,
        far=4,
        scratch=[
            pltpu.VMEM((border_count // 128, 128), integer),
            pltpu.VMEM((1, edges), integer),
            pltpu.VMEM((1, edges), integer),
            pltpu.VMEM((rows, width), BF16),
            pltpu.SemaphoreType.DMA((4,)),
        ],
    )
    asked = lax.all_to_all(request, ("gy", "gz"), split_axis=0, concat_axis=0, tiled=True)
    halo = neighbours(border)

    gain = norm_gain.reshape(1, width)
    q, kv = run(
        project,
        (pltpu.VMEM((rows, width), BF16), pltpu.VMEM((rows, 2 * width), BF16)),
        nodes,
        gain,
        w_qkv,
        far=3,
        scratch=[
            pltpu.VMEM((rows, width), BF16),
            pltpu.VMEM((1, width), F32),
            pltpu.VMEM((width, 3 * width), BF16),
            pltpu.SemaphoreType.DMA((3,)),
        ],
    )
    node_state, answers = run(
        functools.partial(attend, pieces=len(halo)),
        (shape((rows, width), BF16), shape((bricks * capacity, hidden), BF16)),
        block_mask,
        gain,
        w_qkv,
        nodes,
        w_attn_out,
        w_target,
        q,
        kv,
        near(asked),
        *[near(piece) for piece in halo],
        far=6,
        mib=32,
        scratch=[
            pltpu.VMEM((HEADS, rows + len(halo) * border_count, PAIR), BF16),
            pltpu.VMEM(block_mask.shape, integer),
            pltpu.VMEM((1, width), F32),
            pltpu.VMEM((width, 2 * width), BF16),
            pltpu.VMEM((rows, width), BF16),
            pltpu.VMEM((width, width), BF16),
            pltpu.VMEM((width, hidden), BF16),
            pltpu.SemaphoreType.DMA((6,)),
        ],
    )
    answers = lax.all_to_all(
        answers.reshape(bricks, capacity, hidden),
        ("gy", "gz"),
        split_axis=0,
        concat_axis=0,
        tiled=True,
    ).reshape(bricks * capacity, hidden)
    (part,) = run(
        own_part,
        (shape((edges, hidden), F32),),
        edge_source.reshape(edges // 128, 128),
        node_state,
        w_source,
        contact,
        w_contact,
    )
    (scores,) = run(
        score, (shape((1, edges), F32),), place, near(answers), part, w_score.reshape(1, hidden)
    )
    return (node_state, scores.reshape(edges))


def solution(mesh):
    split = ("groups", "gy", "gz")
    in_specs = (
        P(split, None),
        P(split, None),
        P(split),
        P(split, None),
        P(split),
        P(split),
        P(split, None),
        P(),
        P(),
        P(),
        P(),
        P(),
        P(),
        P(),
    )
    out_specs = (P(split, None), P(split))
    return jax.shard_map(local, mesh=mesh, in_specs=in_specs, out_specs=out_specs, check_vma=False)
```

```python
import functools

import jax
import jax.numpy as jnp
from jax import lax
from jax.experimental import pallas as pl
from jax.experimental.pallas import tpu as pltpu
from jax.sharding import PartitionSpec as P

HEADS = 8
HEAD_DIM = 64
BLOCK = 128
PAIR = 2 * HEAD_DIM
F32 = jnp.float32
BF16 = jnp.bfloat16
FAR = pltpu.HBM
NT = (((1,), (1,)), ((), ()))


def dot(lhs, rhs):
    return jnp.dot(lhs, rhs, preferred_element_type=F32)


def dot_nt(lhs, rhs):
    return lax.dot_general(lhs, rhs, NT, preferred_element_type=F32)


def ones_where(condition):
    return jnp.where(condition, 1.0, 0.0).astype(BF16)


def iota(shape, axis):
    return lax.broadcasted_iota(jnp.int32, shape, axis)


def columns_of(rows):
    count, lanes = rows.shape
    if count < 8:
        rows = jnp.concatenate([rows] * (8 // count), 0)
    return jnp.transpose(rows)


def hot_rows(index_rows, size):
    count = index_rows.shape[0]
    columns = columns_of(index_rows)
    lanes = iota((128, size), 1)
    return jnp.concatenate([ones_where(columns[:, r : r + 1] == lanes) for r in range(count)], 0)


def picked(index_rows, table):
    return dot(hot_rows(index_rows, table.shape[0]), table)


def normed_rows(values, gain):
    wide = values.astype(F32)
    mean = jnp.mean(wide * wide, axis=-1, keepdims=True)
    return (wide * lax.rsqrt(mean + 1e-06) * gain).astype(BF16)


def fetch(sources, places, signals):
    copies = [
        pltpu.make_async_copy(source, place, signals.at[i])
        for i, (source, place) in enumerate(zip(sources, places))
    ]
    for copy in copies:
        copy.start()
    return copies


def prepare(*refs, dims):
    border_ref, request_ref, place_ref, nodes_ref, gain_ref, mask_ref, w_ref = refs[7:14]
    ids_ref, owner_ref, target_ref, signals = refs[14:]
    places = (ids_ref, owner_ref, target_ref, nodes_ref, gain_ref, mask_ref, w_ref)
    copies = fetch(refs[:7], places, signals)
    for copy in copies[:3]:
        copy.wait()
    bricks, capacity = dims
    edges = owner_ref.shape[1]
    owner = owner_ref[...]
    target = target_ref[...]
    mine = iota((bricks, edges), 0) == owner
    mine_f = jnp.where(mine, 1.0, 0.0)
    before = ones_where(iota((edges, edges), 0) < iota((edges, edges), 1))
    counts = dot(mine_f.astype(BF16), before)
    slots = jnp.sum(counts * mine_f, axis=0, keepdims=True).astype(jnp.int32)
    place = owner * capacity + slots
    for r in range(edges // 128):
        place_ref[r : r + 1, :] = place[:, r * 128 : (r + 1) * 128]
    at_slot = ones_where(iota((128, edges), 0) == slots)
    high = (mine_f * (target >> 5).astype(F32)).astype(BF16)
    low = (mine_f * (target & 31).astype(F32)).astype(BF16)
    request = dot_nt(high, at_slot) * 32.0 + dot_nt(low, at_slot)
    request_ref[...] = request.astype(jnp.int32)
    border = ids_ref.shape[0] * 128
    hot = hot_rows(ids_ref[...], nodes_ref.shape[0])
    copies[3].wait()
    border_ref[:border, :] = dot(hot, nodes_ref[...]).astype(BF16)
    border_ref[border:, :] = jnp.ones_like(border_ref[border:, :])
    for copy in copies[4:]:
        copy.wait()


def project(nodes_ref, gain_ref, w_ref, q_ref, kv_ref):
    width = nodes_ref.shape[1]
    normed = normed_rows(nodes_ref[...], gain_ref[...])
    scale = 1.4426950408889634 / HEAD_DIM**0.5
    q_ref[...] = (dot(normed, w_ref[:, :width]) * scale).astype(BF16)
    kv_ref[...] = dot(normed, w_ref[:, width:]).astype(BF16)


def attend(*refs, pieces):
    w_out_hbm, w_target_hbm, nodes_ref, gain_ref, mask_ref, w_ref, q_ref, kv_ref = refs[:8]
    halo_refs = refs[8 : 8 + pieces]
    state_ref, table_ref, w_out_ref, w_target_ref, v_ref, signals = refs[8 + pieces :]
    copies = fetch((w_out_hbm, w_target_hbm), (w_out_ref, w_target_ref), signals)
    rows, width = q_ref.shape
    blocks = rows // BLOCK
    keys = v_ref.shape[0] // 2
    border = (keys - rows) // pieces
    halo_nodes = jnp.concatenate([ref[:border, :] for ref in halo_refs], 0)
    halo = dot(normed_rows(halo_nodes, gain_ref[...]), w_ref[:, width:]).astype(BF16)
    low_keys = iota((keys, PAIR), 1) < HEAD_DIM
    low = iota((rows, PAIR), 1) < HEAD_DIM

    lane = iota((blocks, 128), 1)
    row = iota((blocks, 128), 0)
    seen = dot(mask_ref[...].astype(F32).astype(BF16), ones_where(row == lane))
    seen = jnp.where(row == lane, 1.0, seen)
    for h in range(pieces):
        sent = halo_refs[h][border : border + 1, :128].astype(F32)
        seen = jnp.where(lane == blocks + h, sent, seen)
    bias = jnp.where(seen > 0.5, 0.0, -1e30).astype(BF16)
    bias = jnp.concatenate(
        [jnp.broadcast_to(bias[b : b + 1, :], (BLOCK, 128)) for b in range(blocks)], 0
    )
    own = iota((rows, 128), 0) // BLOCK
    far = blocks + iota((keys - rows, 128), 0) // border
    key_block = jnp.concatenate(
        [ones_where(own == iota(own.shape, 1)), ones_where(far == iota(far.shape, 1))], 0
    )
    key_block = jnp.concatenate([key_block, key_block], 0)
    v_ref[:keys, PAIR:] = jnp.zeros((keys, PAIR), BF16)
    v_ref[keys:, :PAIR] = jnp.zeros((keys, PAIR), BF16)

    attended = []
    for pair in range(width // PAIR):
        at = slice(pair * PAIR, (pair + 1) * PAIR)
        v_at = slice(width + pair * PAIR, width + (pair + 1) * PAIR)
        values = jnp.concatenate([kv_ref[:, v_at], halo[:, v_at]], 0)
        one = jnp.ones_like(values)
        v_ref[:keys, :PAIR] = jnp.where(low_keys, values, one)
        v_ref[keys:, PAIR:] = jnp.where(low_keys, one, values)
        k_pair = jnp.concatenate([kv_ref[:, at], halo[:, at]], 0)
        zero = jnp.zeros_like(k_pair)
        k_pair = jnp.concatenate(
            [jnp.where(low_keys, k_pair, zero), jnp.where(low_keys, zero, k_pair)], 0
        )
        k_pair = jnp.concatenate([k_pair, key_block], 1)
        scores = dot_nt(jnp.concatenate([q_ref[:, at], bias], 1), k_pair)
        weights = []
        for half in (scores[:, :keys], scores[:, keys:]):
            fold = half[:, :128]
            for c in range(128, keys, 128):
                fold = jnp.maximum(fold, half[:, c : c + 128])
            top = jnp.max(fold, axis=1, keepdims=True)
            weights.append(jnp.exp2((half - top).astype(BF16)))
        mixed = dot(jnp.concatenate(weights, 1), v_ref[...])
        even, odd = mixed[:, :PAIR], mixed[:, PAIR:]
        total = pltpu.roll(jnp.where(low, odd, even), HEAD_DIM, 1)
        attended.append((jnp.where(low, even, odd) / total).astype(BF16))
    for copy in copies:
        copy.wait()
    state = nodes_ref[...].astype(F32) + dot(jnp.concatenate(attended, 1), w_out_ref[...])
    state = state.astype(BF16)
    state_ref[...] = state
    table_ref[...] = dot(state, w_target_ref[...]).astype(BF16)


def answer(table_hbm, request_ref, answer_ref, table_ref, signals):
    (copy,) = fetch((table_hbm,), (table_ref,), signals)
    bricks = request_ref.shape[0]
    capacity = answer_ref.shape[0] // bricks
    columns = jnp.transpose(request_ref[...])
    lanes = iota((capacity, table_ref.shape[0]), 1)
    hot = [ones_where(columns[:capacity, b : b + 1] == lanes) for b in range(bricks)]
    hot = jnp.concatenate(hot, 0)
    copy.wait()
    answer_ref[...] = dot(hot, table_ref[...]).astype(BF16)


def own_part(
    index_ref, state_ref, w_source_ref, contact_ref, w_ref, part_ref
):
    rows = picked(index_ref[...], state_ref[...]).astype(BF16)
    rows = dot(rows, w_source_ref[...]).astype(BF16).astype(F32)
    part_ref[...] = rows + dot(contact_ref[...], w_ref[...])


def score(place_ref, answers_ref, part_ref, w_ref, out_ref):
    pre = part_ref[...] + picked(place_ref[...], answers_ref[...])
    weighted = jax.nn.gelu(pre) * w_ref[...]
    folded = weighted[:, :128]
    for at in range(128, weighted.shape[1], 128):
        folded = folded + weighted[:, at : at + 128]
    out_ref[...] = jnp.sum(jnp.transpose(folded), axis=0, keepdims=True)


def near(array):
    return pltpu.with_memory_space_constraint(array, pltpu.VMEM)


def away(array):
    return pltpu.with_memory_space_constraint(array, pltpu.HBM)


def run(kernel, outs, *args, scratch=(), mib=16, far=0):
    space = pl.BlockSpec(memory_space=pltpu.VMEM)
    left = pl.BlockSpec(memory_space=FAR)
    args = [away(arg) for arg in args[:far]] + list(args[far:])
    return pl.pallas_call(
        kernel,
        out_shape=tuple(outs),
        in_specs=[left] * far + [space] * (len(args) - far),
        out_specs=(space,) * len(outs),
        scratch_shapes=scratch,
        compiler_params=pltpu.CompilerParams(vmem_limit_bytes=mib * 1024 * 1024),
    )(*args)


def shape(dims, dtype):
    return jax.ShapeDtypeStruct(dims, dtype)


def neighbours(block):
    steps = []
    for axis in ("gy", "gz"):
        count = lax.axis_size(axis)
        for first in range(min(2, count - 1)):
            swaps = []
            for i in range(first, count - 1, 2):
                swaps += [(i, i + 1), (i + 1, i)]
            steps.append((axis, swaps))
    return [lax.ppermute(block, axis, swaps) for axis, swaps in reversed(steps)]


def local(
    nodes,
    block_mask,
    border_ids,
    contact,
    edge_source,
    edge_target,
    edge_owner,
    norm_gain,
    w_qkv,
    w_attn_out,
    w_source,
    w_target,
    w_contact,
    w_score,
):
    rows, width = nodes.shape
    edges = edge_source.shape[0]
    border_count = border_ids.shape[0]
    bricks = lax.axis_size("gy") * lax.axis_size("gz")
    capacity = max(2 * edges // bricks, 2)
    hidden = w_target.shape[1]
    integer = jnp.int32
    border, request, place, nodes_near, gain, mask, w_near = run(
        functools.partial(prepare, dims=(bricks, capacity)),
        (
            shape((border_count + 16, width), BF16),
            shape((bricks, 128), integer),
            shape((edges // 128, 128), integer),
            pltpu.VMEM((rows, width), BF16),
            pltpu.VMEM((1, width), F32),
            pltpu.VMEM(block_mask.shape, integer),
            pltpu.VMEM((width, 3 * width), BF16),
        ),
        border_ids.reshape(border_count // 128, 128),
        edge_owner.reshape(1, edges),
        edge_target.reshape(1, edges),
        nodes,
        norm_gain.reshape(1, width),
        block_mask,
        w_qkv,
        far=7,
        scratch=[
            pltpu.VMEM((border_count // 128, 128), integer),
            pltpu.VMEM((1, edges), integer),
            pltpu.VMEM((1, edges), integer),
            pltpu.SemaphoreType.DMA((7,)),
        ],
    )
    asked = lax.all_to_all(request, ("gy", "gz"), split_axis=0, concat_axis=0, tiled=True)
    halo = neighbours(border)

    q, kv = run(
        project,
        (pltpu.VMEM((rows, width), BF16), pltpu.VMEM((rows, 2 * width), BF16)),
        nodes_near,
        gain,
        w_near,
    )
    keys = rows + len(halo) * border_count
    node_state, table = run(
        functools.partial(attend, pieces=len(halo)),
        (shape((rows, width), BF16), shape((rows, hidden), BF16)),
        w_attn_out,
        w_target,
        nodes_near,
        gain,
        mask,
        w_near,
        q,
        kv,
        *[near(piece) for piece in halo],
        far=2,
        mib=40,
        scratch=[
            pltpu.VMEM((width, width), BF16),
            pltpu.VMEM((width, hidden), BF16),
            pltpu.VMEM((2 * keys, 2 * PAIR), BF16),
            pltpu.SemaphoreType.DMA((2,)),
        ],
    )
    (answers,) = run(
        answer,
        (shape((bricks * capacity, hidden), BF16),),
        table,
        near(asked),
        far=1,
        scratch=[pltpu.VMEM((rows, hidden), BF16), pltpu.SemaphoreType.DMA((1,))],
    )
    answers = lax.all_to_all(
        answers.reshape(bricks, capacity, hidden),
        ("gy", "gz"),
        split_axis=0,
        concat_axis=0,
        tiled=True,
    ).reshape(bricks * capacity, hidden)
    (part,) = run(
        own_part,
        (shape((edges, hidden), F32),),
        edge_source.reshape(edges // 128, 128),
        node_state,
        w_source,
        contact,
        w_contact,
    )
    (scores,) = run(
        score, (shape((1, edges), F32),), place, near(answers), part, w_score.reshape(1, hidden)
    )
    return (node_state, scores.reshape(edges))


def solution(mesh):
    split = ("groups", "gy", "gz")
    in_specs = (
        P(split, None),
        P(split, None),
        P(split),
        P(split, None),
        P(split),
        P(split),
        P(split, None),
        P(),
        P(),
        P(),
        P(),
        P(),
        P(),
        P(),
    )
    out_specs = (P(split, None), P(split))
    return jax.shard_map(local, mesh=mesh, in_specs=in_specs, out_specs=out_specs, check_vma=False)
```

```python
import functools

import jax
import jax.numpy as jnp
from jax import lax
from jax.experimental import pallas as pl
from jax.experimental.pallas import tpu as pltpu
from jax.sharding import PartitionSpec as P

HEADS = 8
HEAD_DIM = 64
BLOCK = 128
PAIR = 2 * HEAD_DIM
F32 = jnp.float32
BF16 = jnp.bfloat16
FAR = pltpu.HBM
NT = (((1,), (1,)), ((), ()))


def dot(lhs, rhs):
    return jnp.dot(lhs, rhs, preferred_element_type=F32)


def dot_nt(lhs, rhs):
    return lax.dot_general(lhs, rhs, NT, preferred_element_type=F32)


def ones_where(condition):
    return jnp.where(condition, 1.0, 0.0).astype(BF16)


def iota(shape, axis):
    return lax.broadcasted_iota(jnp.int32, shape, axis)


def columns_of(rows):
    count, lanes = rows.shape
    if count < 8:
        rows = jnp.concatenate([rows] * (8 // count), 0)
    return jnp.transpose(rows)


def hot_rows(index_rows, size):
    count = index_rows.shape[0]
    columns = columns_of(index_rows)
    lanes = iota((128, size), 1)
    return jnp.concatenate([ones_where(columns[:, r : r + 1] == lanes) for r in range(count)], 0)


def picked(index_rows, table):
    return dot(hot_rows(index_rows, table.shape[0]), table)


def normed_rows(values, gain):
    wide = values.astype(F32)
    mean = jnp.mean(wide * wide, axis=-1, keepdims=True)
    return (wide * lax.rsqrt(mean + 1e-06) * gain).astype(BF16)


def fetch(sources, places, signals):
    copies = [
        pltpu.make_async_copy(source, place, signals.at[i])
        for i, (source, place) in enumerate(zip(sources, places))
    ]
    for copy in copies:
        copy.start()
    return copies


def prepare(*refs, dims):
    border_ref, request_ref, place_ref, nodes_ref, gain_ref, mask_ref, w_ref = refs[7:14]
    ids_ref, owner_ref, target_ref, signals = refs[14:]
    places = (ids_ref, owner_ref, target_ref, nodes_ref, gain_ref, mask_ref, w_ref)
    copies = fetch(refs[:7], places, signals)
    for copy in copies[:3]:
        copy.wait()
    bricks, capacity = dims
    edges = owner_ref.shape[1]
    owner = owner_ref[...]
    target = target_ref[...]
    mine = iota((bricks, edges), 0) == owner
    mine_f = jnp.where(mine, 1.0, 0.0)
    before = ones_where(iota((edges, edges), 0) < iota((edges, edges), 1))
    counts = dot(mine_f.astype(BF16), before)
    slots = jnp.sum(counts * mine_f, axis=0, keepdims=True).astype(jnp.int32)
    place = owner * capacity + slots
    for r in range(edges // 128):
        place_ref[r : r + 1, :] = place[:, r * 128 : (r + 1) * 128]
    at_slot = ones_where(iota((128, edges), 0) == slots)
    high = (mine_f * (target >> 5).astype(F32)).astype(BF16)
    low = (mine_f * (target & 31).astype(F32)).astype(BF16)
    request = dot_nt(high, at_slot) * 32.0 + dot_nt(low, at_slot)
    request_ref[...] = request.astype(jnp.int32)
    border = ids_ref.shape[0] * 128
    hot = hot_rows(ids_ref[...], nodes_ref.shape[0])
    copies[3].wait()
    border_ref[:border, :] = dot(hot, nodes_ref[...]).astype(BF16)
    border_ref[border:, :] = jnp.ones_like(border_ref[border:, :])
    for copy in copies[4:]:
        copy.wait()


def project(nodes_ref, gain_ref, w_ref, q_ref, kv_ref):
    width = nodes_ref.shape[1]
    normed = normed_rows(nodes_ref[...], gain_ref[...])
    scale = 1.4426950408889634 / HEAD_DIM**0.5
    q_ref[...] = (dot(normed, w_ref[:, :width]) * scale).astype(BF16)
    kv_ref[...] = dot(normed, w_ref[:, width:]).astype(BF16)


def attend(*refs, pieces):
    w_out_hbm, w_target_hbm, nodes_hbm, gain_ref, mask_ref, w_ref, q_ref, kv_ref = refs[:8]
    halo_refs = refs[8 : 8 + pieces]
    state_hbm, table_ref, w_out_ref, w_target_ref, nodes_ref, v_ref, signals, sent = refs[
        8 + pieces :
    ]
    copies = fetch(
        (w_out_hbm, w_target_hbm, nodes_hbm), (w_out_ref, w_target_ref, nodes_ref), signals
    )
    rows, width = q_ref.shape
    blocks = rows // BLOCK
    keys = v_ref.shape[0] // 2
    border = (keys - rows) // pieces
    halo_nodes = jnp.concatenate([ref[:border, :] for ref in halo_refs], 0)
    halo = dot(normed_rows(halo_nodes, gain_ref[...]), w_ref[:, width:]).astype(BF16)
    low_keys = iota((keys, PAIR), 1) < HEAD_DIM
    low = iota((rows, PAIR), 1) < HEAD_DIM

    lane = iota((blocks, 128), 1)
    row = iota((blocks, 128), 0)
    seen = dot(mask_ref[...].astype(F32).astype(BF16), ones_where(row == lane))
    seen = jnp.where(row == lane, 1.0, seen)
    for h in range(pieces):
        marker = halo_refs[h][border : border + 1, :128].astype(F32)
        seen = jnp.where(lane == blocks + h, marker, seen)
    bias = jnp.where(seen > 0.5, 0.0, -1e30).astype(BF16)
    bias = jnp.concatenate(
        [jnp.broadcast_to(bias[b : b + 1, :], (BLOCK, 128)) for b in range(blocks)], 0
    )
    own = iota((rows, 128), 0) // BLOCK
    far = blocks + iota((keys - rows, 128), 0) // border
    key_block = jnp.concatenate(
        [ones_where(own == iota(own.shape, 1)), ones_where(far == iota(far.shape, 1))], 0
    )
    key_block = jnp.concatenate([key_block, key_block], 0)
    v_ref[:keys, PAIR:] = jnp.zeros((keys, PAIR), BF16)
    v_ref[keys:, :PAIR] = jnp.zeros((keys, PAIR), BF16)

    attended = []
    for pair in range(width // PAIR):
        at = slice(pair * PAIR, (pair + 1) * PAIR)
        v_at = slice(width + pair * PAIR, width + (pair + 1) * PAIR)
        values = jnp.concatenate([kv_ref[:, v_at], halo[:, v_at]], 0)
        one = jnp.ones_like(values)
        v_ref[:keys, :PAIR] = jnp.where(low_keys, values, one)
        v_ref[keys:, PAIR:] = jnp.where(low_keys, one, values)
        k_pair = jnp.concatenate([kv_ref[:, at], halo[:, at]], 0)
        zero = jnp.zeros_like(k_pair)
        k_pair = jnp.concatenate(
            [jnp.where(low_keys, k_pair, zero), jnp.where(low_keys, zero, k_pair)], 0
        )
        k_pair = jnp.concatenate([k_pair, key_block], 1)
        scores = dot_nt(jnp.concatenate([q_ref[:, at], bias], 1), k_pair)
        weights = []
        for half in (scores[:, :keys], scores[:, keys:]):
            fold = half[:, :128]
            for c in range(128, keys, 128):
                fold = jnp.maximum(fold, half[:, c : c + 128])
            top = jnp.max(fold, axis=1, keepdims=True)
            weights.append(jnp.exp2((half - top).astype(BF16)))
        mixed = dot(jnp.concatenate(weights, 1), v_ref[...])
        even, odd = mixed[:, :PAIR], mixed[:, PAIR:]
        total = pltpu.roll(jnp.where(low, odd, even), HEAD_DIM, 1)
        attended.append((jnp.where(low, even, odd) / total).astype(BF16))
    for copy in copies:
        copy.wait()
    state = nodes_ref[...].astype(F32) + dot(jnp.concatenate(attended, 1), w_out_ref[...])
    state = state.astype(BF16)
    nodes_ref[...] = state
    out = pltpu.make_async_copy(nodes_ref, state_hbm, sent)
    out.start()
    table_ref[...] = dot(state, w_target_ref[...]).astype(BF16)
    out.wait()


def answer(request_ref, table_ref, answer_hbm, answer_ref, sent):
    bricks = request_ref.shape[0]
    capacity = answer_ref.shape[0] // bricks
    columns = jnp.transpose(request_ref[...])
    lanes = iota((capacity, table_ref.shape[0]), 1)
    copies = []
    for first in range(0, bricks, bricks // 4):
        hot = [
            ones_where(columns[:capacity, b : b + 1] == lanes)
            for b in range(first, first + bricks // 4)
        ]
        at = pl.ds(first * capacity, bricks // 4 * capacity)
        answer_ref[at, :] = dot(jnp.concatenate(hot, 0), table_ref[...]).astype(BF16)
        copies.append(
            pltpu.make_async_copy(
                answer_ref.at[at], answer_hbm.at[at], sent.at[first // (bricks // 4)]
            )
        )
        copies[-1].start()
    for copy in copies:
        copy.wait()


def own_part(
    index_ref, state_ref, w_source_ref, contact_ref, w_ref, part_ref
):
    rows = picked(index_ref[...], state_ref[...]).astype(BF16)
    rows = dot(rows, w_source_ref[...]).astype(BF16).astype(F32)
    part_ref[...] = rows + dot(contact_ref[...], w_ref[...])


def score(place_ref, answers_ref, part_ref, w_ref, out_ref):
    pre = part_ref[...] + picked(place_ref[...], answers_ref[...])
    weighted = jax.nn.gelu(pre) * w_ref[...]
    folded = weighted[:, :128]
    for at in range(128, weighted.shape[1], 128):
        folded = folded + weighted[:, at : at + 128]
    out_ref[...] = jnp.sum(jnp.transpose(folded), axis=0, keepdims=True)


def near(array):
    return pltpu.with_memory_space_constraint(array, pltpu.VMEM)


def away(array):
    return pltpu.with_memory_space_constraint(array, pltpu.HBM)


def run(kernel, outs, *args, scratch=(), mib=16, far=0, far_outs=0):
    space = pl.BlockSpec(memory_space=pltpu.VMEM)
    left = pl.BlockSpec(memory_space=FAR)
    args = [away(arg) for arg in args[:far]] + list(args[far:])
    return pl.pallas_call(
        kernel,
        out_shape=tuple(outs),
        in_specs=[left] * far + [space] * (len(args) - far),
        out_specs=(left,) * far_outs + (space,) * (len(outs) - far_outs),
        scratch_shapes=scratch,
        compiler_params=pltpu.CompilerParams(vmem_limit_bytes=mib * 1024 * 1024),
    )(*args)


def shape(dims, dtype):
    return jax.ShapeDtypeStruct(dims, dtype)


def neighbours(block):
    steps = []
    for axis in ("gy", "gz"):
        count = lax.axis_size(axis)
        for first in range(min(2, count - 1)):
            swaps = []
            for i in range(first, count - 1, 2):
                swaps += [(i, i + 1), (i + 1, i)]
            steps.append((axis, swaps))
    return [lax.ppermute(block, axis, swaps) for axis, swaps in reversed(steps)]


def local(
    nodes,
    block_mask,
    border_ids,
    contact,
    edge_source,
    edge_target,
    edge_owner,
    norm_gain,
    w_qkv,
    w_attn_out,
    w_source,
    w_target,
    w_contact,
    w_score,
):
    rows, width = nodes.shape
    edges = edge_source.shape[0]
    border_count = border_ids.shape[0]
    bricks = lax.axis_size("gy") * lax.axis_size("gz")
    capacity = max(2 * edges // bricks, 2)
    hidden = w_target.shape[1]
    integer = jnp.int32
    border, request, place, nodes_near, gain, mask, w_near = run(
        functools.partial(prepare, dims=(bricks, capacity)),
        (
            shape((border_count + 16, width), BF16),
            shape((bricks, 128), integer),
            shape((edges // 128, 128), integer),
            pltpu.VMEM((rows, width), BF16),
            pltpu.VMEM((1, width), F32),
            pltpu.VMEM(block_mask.shape, integer),
            pltpu.VMEM((width, 3 * width), BF16),
        ),
        border_ids.reshape(border_count // 128, 128),
        edge_owner.reshape(1, edges),
        edge_target.reshape(1, edges),
        nodes,
        norm_gain.reshape(1, width),
        block_mask,
        w_qkv,
        far=7,
        scratch=[
            pltpu.VMEM((border_count // 128, 128), integer),
            pltpu.VMEM((1, edges), integer),
            pltpu.VMEM((1, edges), integer),
            pltpu.SemaphoreType.DMA((7,)),
        ],
    )
    asked = lax.all_to_all(request, ("gy", "gz"), split_axis=0, concat_axis=0, tiled=True)
    halo = neighbours(border)

    q, kv = run(
        project,
        (pltpu.VMEM((rows, width), BF16), pltpu.VMEM((rows, 2 * width), BF16)),
        nodes_near,
        gain,
        w_near,
    )
    keys = rows + len(halo) * border_count
    node_state, table = run(
        functools.partial(attend, pieces=len(halo)),
        (shape((rows, width), BF16), pltpu.VMEM((rows, hidden), BF16)),
        w_attn_out,
        w_target,
        nodes,
        gain,
        mask,
        w_near,
        q,
        kv,
        *[near(piece) for piece in halo],
        far=3,
        mib=40,
        scratch=[
            pltpu.VMEM((width, width), BF16),
            pltpu.VMEM((width, hidden), BF16),
            pltpu.VMEM((rows, width), BF16),
            pltpu.VMEM((2 * keys, 2 * PAIR), BF16),
            pltpu.SemaphoreType.DMA((3,)),
            pltpu.SemaphoreType.DMA,
        ],
        far_outs=1,
    )
    (answers,) = run(
        answer,
        (shape((bricks * capacity, hidden), BF16),),
        near(asked),
        table,
        scratch=[
            pltpu.VMEM((bricks * capacity, hidden), BF16),
            pltpu.SemaphoreType.DMA((4,)),
        ],
        far_outs=1,
    )
    answers = lax.all_to_all(
        answers.reshape(bricks, capacity, hidden),
        ("gy", "gz"),
        split_axis=0,
        concat_axis=0,
        tiled=True,
    ).reshape(bricks * capacity, hidden)
    (part,) = run(
        own_part,
        (pltpu.VMEM((edges, hidden), F32),),
        edge_source.reshape(edges // 128, 128),
        node_state,
        w_source,
        contact,
        w_contact,
    )
    (scores,) = run(
        score, (shape((1, edges), F32),), place, near(answers), part, w_score.reshape(1, hidden)
    )
    return (node_state, scores.reshape(edges))


def solution(mesh):
    split = ("groups", "gy", "gz")
    in_specs = (
        P(split, None),
        P(split, None),
        P(split),
        P(split, None),
        P(split),
        P(split),
        P(split, None),
        P(),
        P(),
        P(),
        P(),
        P(),
        P(),
        P(),
    )
    out_specs = (P(split, None), P(split))
    return jax.shard_map(local, mesh=mesh, in_specs=in_specs, out_specs=out_specs, check_vma=False)
```

```python
import functools

import jax
import jax.numpy as jnp
from jax import lax
from jax.experimental import pallas as pl
from jax.experimental.pallas import tpu as pltpu
from jax.sharding import PartitionSpec as P

HEADS = 8
HEAD_DIM = 64
BLOCK = 128
PAIR = 2 * HEAD_DIM
F32 = jnp.float32
BF16 = jnp.bfloat16
FAR = pltpu.HBM
NT = (((1,), (1,)), ((), ()))


def dot(lhs, rhs):
    return jnp.dot(lhs, rhs, preferred_element_type=F32)


def dot_nt(lhs, rhs):
    return lax.dot_general(lhs, rhs, NT, preferred_element_type=F32)


def ones_where(condition):
    return jnp.where(condition, 1.0, 0.0).astype(BF16)


def iota(shape, axis):
    return lax.broadcasted_iota(jnp.int32, shape, axis)


def columns_of(rows):
    count, lanes = rows.shape
    if count < 8:
        rows = jnp.concatenate([rows] * (8 // count), 0)
    return jnp.transpose(rows)


def hot_rows(index_rows, size):
    count = index_rows.shape[0]
    columns = columns_of(index_rows)
    lanes = iota((128, size), 1)
    return jnp.concatenate([ones_where(columns[:, r : r + 1] == lanes) for r in range(count)], 0)


def picked(index_rows, table):
    return dot(hot_rows(index_rows, table.shape[0]), table)


def normed_rows(values, gain):
    wide = values.astype(F32)
    mean = jnp.mean(wide * wide, axis=-1, keepdims=True)
    return (wide * lax.rsqrt(mean + 1e-06) * gain).astype(BF16)


def fetch(sources, places, signals):
    copies = [
        pltpu.make_async_copy(source, place, signals.at[i])
        for i, (source, place) in enumerate(zip(sources, places))
    ]
    for copy in copies:
        copy.start()
    return copies


def prepare(*refs, dims):
    border_ref, request_ref, place_ref, nodes_ref, gain_ref, mask_ref, w_ref = refs[7:14]
    ids_ref, owner_ref, target_ref, signals = refs[14:]
    places = (ids_ref, owner_ref, target_ref, nodes_ref, gain_ref, mask_ref, w_ref)
    copies = fetch(refs[:7], places, signals)
    for copy in copies[:3]:
        copy.wait()
    bricks, capacity = dims
    edges = owner_ref.shape[1]
    owner = owner_ref[...]
    target = target_ref[...]
    mine = iota((bricks, edges), 0) == owner
    mine_f = jnp.where(mine, 1.0, 0.0)
    before = ones_where(iota((edges, edges), 0) < iota((edges, edges), 1))
    counts = dot(mine_f.astype(BF16), before)
    slots = jnp.sum(counts * mine_f, axis=0, keepdims=True).astype(jnp.int32)
    place = owner * capacity + slots
    for r in range(edges // 128):
        place_ref[r : r + 1, :] = place[:, r * 128 : (r + 1) * 128]
    at_slot = ones_where(iota((128, edges), 0) == slots)
    high = (mine_f * (target >> 5).astype(F32)).astype(BF16)
    low = (mine_f * (target & 31).astype(F32)).astype(BF16)
    request = dot_nt(high, at_slot) * 32.0 + dot_nt(low, at_slot)
    request_ref[...] = request.astype(jnp.int32)
    border = ids_ref.shape[0] * 128
    hot = hot_rows(ids_ref[...], nodes_ref.shape[0])
    copies[3].wait()
    border_ref[:border, :] = dot(hot, nodes_ref[...]).astype(BF16)
    border_ref[border:, :] = jnp.ones_like(border_ref[border:, :])
    for copy in copies[4:]:
        copy.wait()


def project(nodes_ref, gain_ref, w_ref, q_ref, kv_ref):
    width = nodes_ref.shape[1]
    normed = normed_rows(nodes_ref[...], gain_ref[...])
    scale = 1.4426950408889634 / HEAD_DIM**0.5
    q_ref[...] = (dot(normed, w_ref[:, :width]) * scale).astype(BF16)
    kv_ref[...] = dot(normed, w_ref[:, width:]).astype(BF16)


def attend(*refs, pieces):
    w_out_hbm, w_target_hbm, nodes_hbm, gain_ref, mask_ref, w_ref, q_ref, kv_ref = refs[:8]
    halo_refs = refs[8 : 8 + pieces]
    state_hbm, table_ref, w_out_ref, w_target_ref, nodes_ref = refs[8 + pieces : 13 + pieces]
    mixed_ref, v_ref, signals, sent = refs[13 + pieces :]
    copies = fetch(
        (w_out_hbm, w_target_hbm, nodes_hbm), (w_out_ref, w_target_ref, nodes_ref), signals
    )
    rows, width = q_ref.shape
    blocks = rows // BLOCK
    keys = v_ref.shape[1] // 2
    border = (keys - rows) // pieces
    halo_nodes = jnp.concatenate([ref[:border, :] for ref in halo_refs], 0)
    halo = dot(normed_rows(halo_nodes, gain_ref[...]), w_ref[:, width:]).astype(BF16)
    low_keys = iota((keys, PAIR), 1) < HEAD_DIM
    span = rows // 2
    low = iota((span, PAIR), 1) < HEAD_DIM

    lane = iota((blocks, 128), 1)
    row = iota((blocks, 128), 0)
    seen = dot(mask_ref[...].astype(F32).astype(BF16), ones_where(row == lane))
    seen = jnp.where(row == lane, 1.0, seen)
    for h in range(pieces):
        marker = halo_refs[h][border : border + 1, :128].astype(F32)
        seen = jnp.where(lane == blocks + h, marker, seen)
    bias = jnp.where(seen > 0.5, 0.0, -1e30).astype(BF16)
    bias = jnp.concatenate(
        [jnp.broadcast_to(bias[b : b + 1, :], (BLOCK, 128)) for b in range(blocks)], 0
    )
    own = iota((rows, 128), 0) // BLOCK
    far = blocks + iota((keys - rows, 128), 0) // border
    key_block = jnp.concatenate(
        [ones_where(own == iota(own.shape, 1)), ones_where(far == iota(far.shape, 1))], 0
    )
    key_block = jnp.concatenate([key_block, key_block], 0)
    for buffer in range(2):
        v_ref[buffer, :keys, PAIR:] = jnp.zeros((keys, PAIR), BF16)
        v_ref[buffer, keys:, :PAIR] = jnp.zeros((keys, PAIR), BF16)

    def scores_of(pair, part):
        at = slice(pair * PAIR, (pair + 1) * PAIR)
        span_at = slice(part * span, (part + 1) * span)
        k_pair = jnp.concatenate([kv_ref[:, at], halo[:, at]], 0)
        zero = jnp.zeros_like(k_pair)
        k_pair = jnp.concatenate(
            [jnp.where(low_keys, k_pair, zero), jnp.where(low_keys, zero, k_pair)], 0
        )
        k_pair = jnp.concatenate([k_pair, key_block], 1)
        return dot_nt(jnp.concatenate([q_ref[span_at, at], bias[span_at]], 1), k_pair)

    units = [(pair, part) for pair in range(width // PAIR) for part in range(2)]
    following = scores_of(*units[0])
    for step, (pair, part) in enumerate(units):
        scores = following
        if part == 0:
            v_at = slice(width + pair * PAIR, width + (pair + 1) * PAIR)
            values = jnp.concatenate([kv_ref[:, v_at], halo[:, v_at]], 0)
            one = jnp.ones_like(values)
            v_ref[pair % 2, :keys, :PAIR] = jnp.where(low_keys, values, one)
            v_ref[pair % 2, keys:, PAIR:] = jnp.where(low_keys, one, values)
        if step + 1 < len(units):
            following = scores_of(*units[step + 1])
        weights = []
        for half in (scores[:, :keys], scores[:, keys:]):
            fold = half[:, :128]
            for c in range(128, keys, 128):
                fold = jnp.maximum(fold, half[:, c : c + 128])
            top = jnp.max(fold, axis=1, keepdims=True)
            weights.append(jnp.exp2((half - top).astype(BF16)))
        mixed = dot(jnp.concatenate(weights, 1), v_ref[pair % 2])
        even, odd = mixed[:, :PAIR], mixed[:, PAIR:]
        total = pltpu.roll(jnp.where(low, odd, even), HEAD_DIM, 1)
        mixed_ref[part * span : (part + 1) * span, pair * PAIR : (pair + 1) * PAIR] = (
            jnp.where(low, even, odd) / total
        ).astype(BF16)
    for copy in copies:
        copy.wait()
    state = nodes_ref[...].astype(F32) + dot(mixed_ref[...], w_out_ref[...])
    state = state.astype(BF16)
    nodes_ref[...] = state
    out = pltpu.make_async_copy(nodes_ref, state_hbm, sent)
    out.start()
    table_ref[...] = dot(state, w_target_ref[...]).astype(BF16)
    out.wait()


def answer(request_ref, table_ref, answer_hbm, answer_ref, sent):
    bricks = request_ref.shape[0]
    capacity = answer_ref.shape[0] // bricks
    columns = jnp.transpose(request_ref[...])
    lanes = iota((capacity, table_ref.shape[0]), 1)
    copies = []
    for first in range(0, bricks, bricks // 4):
        hot = [
            ones_where(columns[:capacity, b : b + 1] == lanes)
            for b in range(first, first + bricks // 4)
        ]
        at = pl.ds(first * capacity, bricks // 4 * capacity)
        answer_ref[at, :] = dot(jnp.concatenate(hot, 0), table_ref[...]).astype(BF16)
        copies.append(
            pltpu.make_async_copy(
                answer_ref.at[at], answer_hbm.at[at], sent.at[first // (bricks // 4)]
            )
        )
        copies[-1].start()
    for copy in copies:
        copy.wait()


def own_part(
    index_ref, state_ref, w_source_ref, contact_ref, w_ref, part_ref
):
    rows = picked(index_ref[...], state_ref[...]).astype(BF16)
    rows = dot(rows, w_source_ref[...]).astype(BF16).astype(F32)
    part_ref[...] = rows + dot(contact_ref[...], w_ref[...])


def score(place_ref, answers_ref, part_ref, w_ref, out_ref):
    pre = part_ref[...] + picked(place_ref[...], answers_ref[...])
    weighted = jax.nn.gelu(pre) * w_ref[...]
    folded = weighted[:, :128]
    for at in range(128, weighted.shape[1], 128):
        folded = folded + weighted[:, at : at + 128]
    out_ref[...] = jnp.sum(jnp.transpose(folded), axis=0, keepdims=True)


def near(array):
    return pltpu.with_memory_space_constraint(array, pltpu.VMEM)


def away(array):
    return pltpu.with_memory_space_constraint(array, pltpu.HBM)


def run(kernel, outs, *args, scratch=(), mib=16, far=0, far_outs=0):
    space = pl.BlockSpec(memory_space=pltpu.VMEM)
    left = pl.BlockSpec(memory_space=FAR)
    args = [away(arg) for arg in args[:far]] + list(args[far:])
    return pl.pallas_call(
        kernel,
        out_shape=tuple(outs),
        in_specs=[left] * far + [space] * (len(args) - far),
        out_specs=(left,) * far_outs + (space,) * (len(outs) - far_outs),
        scratch_shapes=scratch,
        compiler_params=pltpu.CompilerParams(vmem_limit_bytes=mib * 1024 * 1024),
    )(*args)


def shape(dims, dtype):
    return jax.ShapeDtypeStruct(dims, dtype)


def neighbours(block):
    steps = []
    for axis in ("gy", "gz"):
        count = lax.axis_size(axis)
        for first in range(min(2, count - 1)):
            swaps = []
            for i in range(first, count - 1, 2):
                swaps += [(i, i + 1), (i + 1, i)]
            steps.append((axis, swaps))
    return [lax.ppermute(block, axis, swaps) for axis, swaps in reversed(steps)]


def local(
    nodes,
    block_mask,
    border_ids,
    contact,
    edge_source,
    edge_target,
    edge_owner,
    norm_gain,
    w_qkv,
    w_attn_out,
    w_source,
    w_target,
    w_contact,
    w_score,
):
    rows, width = nodes.shape
    edges = edge_source.shape[0]
    border_count = border_ids.shape[0]
    bricks = lax.axis_size("gy") * lax.axis_size("gz")
    capacity = max(2 * edges // bricks, 2)
    hidden = w_target.shape[1]
    integer = jnp.int32
    border, request, place, nodes_near, gain, mask, w_near = run(
        functools.partial(prepare, dims=(bricks, capacity)),
        (
            shape((border_count + 16, width), BF16),
            shape((bricks, 128), integer),
            shape((edges // 128, 128), integer),
            pltpu.VMEM((rows, width), BF16),
            pltpu.VMEM((1, width), F32),
            pltpu.VMEM(block_mask.shape, integer),
            pltpu.VMEM((width, 3 * width), BF16),
        ),
        border_ids.reshape(border_count // 128, 128),
        edge_owner.reshape(1, edges),
        edge_target.reshape(1, edges),
        nodes,
        norm_gain.reshape(1, width),
        block_mask,
        w_qkv,
        far=7,
        scratch=[
            pltpu.VMEM((border_count // 128, 128), integer),
            pltpu.VMEM((1, edges), integer),
            pltpu.VMEM((1, edges), integer),
            pltpu.SemaphoreType.DMA((7,)),
        ],
    )
    asked = lax.all_to_all(request, ("gy", "gz"), split_axis=0, concat_axis=0, tiled=True)
    halo = neighbours(border)

    q, kv = run(
        project,
        (pltpu.VMEM((rows, width), BF16), pltpu.VMEM((rows, 2 * width), BF16)),
        nodes_near,
        gain,
        w_near,
    )
    keys = rows + len(halo) * border_count
    node_state, table = run(
        functools.partial(attend, pieces=len(halo)),
        (shape((rows, width), BF16), pltpu.VMEM((rows, hidden), BF16)),
        w_attn_out,
        w_target,
        nodes,
        gain,
        mask,
        w_near,
        q,
        kv,
        *[near(piece) for piece in halo],
        far=3,
        mib=40,
        scratch=[
            pltpu.VMEM((width, width), BF16),
            pltpu.VMEM((width, hidden), BF16),
            pltpu.VMEM((rows, width), BF16),
            pltpu.VMEM((rows, width), BF16),
            pltpu.VMEM((2, 2 * keys, 2 * PAIR), BF16),
            pltpu.SemaphoreType.DMA((3,)),
            pltpu.SemaphoreType.DMA,
        ],
        far_outs=1,
    )
    (answers,) = run(
        answer,
        (shape((bricks * capacity, hidden), BF16),),
        near(asked),
        table,
        scratch=[
            pltpu.VMEM((bricks * capacity, hidden), BF16),
            pltpu.SemaphoreType.DMA((4,)),
        ],
        far_outs=1,
    )
    answers = lax.all_to_all(
        answers.reshape(bricks, capacity, hidden),
        ("gy", "gz"),
        split_axis=0,
        concat_axis=0,
        tiled=True,
    ).reshape(bricks * capacity, hidden)
    (part,) = run(
        own_part,
        (pltpu.VMEM((edges, hidden), F32),),
        edge_source.reshape(edges // 128, 128),
        node_state,
        w_source,
        contact,
        w_contact,
    )
    (scores,) = run(
        score, (shape((1, edges), F32),), place, near(answers), part, w_score.reshape(1, hidden)
    )
    return (node_state, scores.reshape(edges))


def solution(mesh):
    split = ("groups", "gy", "gz")
    in_specs = (
        P(split, None),
        P(split, None),
        P(split),
        P(split, None),
        P(split),
        P(split),
        P(split, None),
        P(),
        P(),
        P(),
        P(),
        P(),
        P(),
        P(),
    )
    out_specs = (P(split, None), P(split))
    return jax.shard_map(local, mesh=mesh, in_specs=in_specs, out_specs=out_specs, check_vma=False)
```

```python
import functools

import jax
import jax.numpy as jnp
from jax import lax
from jax.experimental import pallas as pl
from jax.experimental.pallas import tpu as pltpu
from jax.sharding import PartitionSpec as P

HEADS = 8
HEAD_DIM = 64
BLOCK = 128
PAIR = 2 * HEAD_DIM
F32 = jnp.float32
BF16 = jnp.bfloat16
FAR = pltpu.HBM
NT = (((1,), (1,)), ((), ()))


def dot(lhs, rhs):
    return jnp.dot(lhs, rhs, preferred_element_type=F32)


def dot_nt(lhs, rhs):
    return lax.dot_general(lhs, rhs, NT, preferred_element_type=F32)


def ones_where(condition):
    return jnp.where(condition, 1.0, 0.0).astype(BF16)


def iota(shape, axis):
    return lax.broadcasted_iota(jnp.int32, shape, axis)


def columns_of(rows):
    count, lanes = rows.shape
    if count < 8:
        rows = jnp.concatenate([rows] * (8 // count), 0)
    return jnp.transpose(rows)


def hot_rows(index_rows, size):
    count = index_rows.shape[0]
    columns = columns_of(index_rows)
    lanes = iota((128, size), 1)
    return jnp.concatenate([ones_where(columns[:, r : r + 1] == lanes) for r in range(count)], 0)


def picked(index_rows, table):
    return dot(hot_rows(index_rows, table.shape[0]), table)


def normed_rows(values, gain):
    wide = values.astype(F32)
    mean = jnp.mean(wide * wide, axis=-1, keepdims=True)
    return (wide * lax.rsqrt(mean + 1e-06) * gain).astype(BF16)


def fetch(sources, places, signals):
    copies = [
        pltpu.make_async_copy(source, place, signals.at[i])
        for i, (source, place) in enumerate(zip(sources, places))
    ]
    for copy in copies:
        copy.start()
    return copies


def prepare(*refs, dims):
    border_ref, request_ref, place_ref, nodes_ref, gain_ref, mask_ref, w_ref = refs[7:14]
    ids_ref, owner_ref, target_ref, signals = refs[14:]
    places = (ids_ref, owner_ref, target_ref, nodes_ref, gain_ref, mask_ref, w_ref)
    copies = fetch(refs[:7], places, signals)
    for copy in copies[:3]:
        copy.wait()
    bricks, capacity = dims
    edges = owner_ref.shape[1]
    owner = owner_ref[...]
    target = target_ref[...]
    mine = iota((bricks, edges), 0) == owner
    mine_f = jnp.where(mine, 1.0, 0.0)
    before = ones_where(iota((edges, edges), 0) < iota((edges, edges), 1))
    counts = dot(mine_f.astype(BF16), before)
    slots = jnp.sum(counts * mine_f, axis=0, keepdims=True).astype(jnp.int32)
    place = owner * capacity + slots
    for r in range(edges // 128):
        place_ref[r : r + 1, :] = place[:, r * 128 : (r + 1) * 128]
    at_slot = ones_where(iota((128, edges), 0) == slots)
    high = (mine_f * (target >> 5).astype(F32)).astype(BF16)
    low = (mine_f * (target & 31).astype(F32)).astype(BF16)
    request = dot_nt(high, at_slot) * 32.0 + dot_nt(low, at_slot)
    request_ref[...] = request.astype(jnp.int32)
    border = ids_ref.shape[0] * 128
    hot = hot_rows(ids_ref[...], nodes_ref.shape[0])
    copies[3].wait()
    border_ref[:border, :] = dot(hot, nodes_ref[...]).astype(BF16)
    border_ref[border:, :] = jnp.ones_like(border_ref[border:, :])
    for copy in copies[4:]:
        copy.wait()


def project(nodes_ref, gain_ref, w_ref, q_ref, kv_ref):
    width = nodes_ref.shape[1]
    normed = normed_rows(nodes_ref[...], gain_ref[...])
    scale = 1.4426950408889634 / HEAD_DIM**0.5
    q_ref[...] = (dot(normed, w_ref[:, :width]) * scale).astype(BF16)
    kv_ref[...] = dot(normed, w_ref[:, width:]).astype(BF16)


def attend(*refs, pieces):
    w_out_hbm, w_target_hbm, nodes_hbm, gain_ref, mask_ref, w_ref, q_ref, kv_ref = refs[:8]
    halo_refs = refs[8 : 8 + pieces]
    state_hbm, table_ref, w_out_ref, w_target_ref, nodes_ref = refs[8 + pieces : 13 + pieces]
    mixed_ref, v_ref, signals, sent = refs[13 + pieces :]
    copies = fetch(
        (w_out_hbm, w_target_hbm, nodes_hbm), (w_out_ref, w_target_ref, nodes_ref), signals
    )
    rows, width = q_ref.shape
    blocks = rows // BLOCK
    keys = v_ref.shape[1] // 2
    border = (keys - rows) // pieces
    halo_nodes = jnp.concatenate([ref[:border, :] for ref in halo_refs], 0)
    halo = dot(normed_rows(halo_nodes, gain_ref[...]), w_ref[:, width:]).astype(BF16)
    low_keys = iota((keys, PAIR), 1) < HEAD_DIM
    span = rows // 2
    low = iota((span, PAIR), 1) < HEAD_DIM

    lane = iota((blocks, 128), 1)
    row = iota((blocks, 128), 0)
    seen = dot(mask_ref[...].astype(F32).astype(BF16), ones_where(row == lane))
    seen = jnp.where(row == lane, 1.0, seen)
    for h in range(pieces):
        marker = halo_refs[h][border : border + 1, :128].astype(F32)
        seen = jnp.where(lane == blocks + h, marker, seen)
    bias = jnp.where(seen > 0.5, 0.0, -1e30).astype(BF16)
    bias = jnp.concatenate(
        [jnp.broadcast_to(bias[b : b + 1, :], (BLOCK, 128)) for b in range(blocks)], 0
    )
    own = iota((rows, 128), 0) // BLOCK
    far = blocks + iota((keys - rows, 128), 0) // border
    key_block = jnp.concatenate(
        [ones_where(own == iota(own.shape, 1)), ones_where(far == iota(far.shape, 1))], 0
    )
    key_block = jnp.concatenate([key_block, key_block], 0)
    for buffer in range(2):
        v_ref[buffer, :keys, PAIR:] = jnp.zeros((keys, PAIR), BF16)
        v_ref[buffer, keys:, :PAIR] = jnp.zeros((keys, PAIR), BF16)

    def scores_of(pair, part):
        at = slice(pair * PAIR, (pair + 1) * PAIR)
        span_at = slice(part * span, (part + 1) * span)
        k_pair = jnp.concatenate([kv_ref[:, at], halo[:, at]], 0)
        zero = jnp.zeros_like(k_pair)
        k_pair = jnp.concatenate(
            [jnp.where(low_keys, k_pair, zero), jnp.where(low_keys, zero, k_pair)], 0
        )
        k_pair = jnp.concatenate([k_pair, key_block], 1)
        return dot_nt(jnp.concatenate([q_ref[span_at, at], bias[span_at]], 1), k_pair)

    units = [(pair, part) for pair in range(width // PAIR) for part in range(2)]
    following = scores_of(*units[0])
    for step, (pair, part) in enumerate(units):
        scores = following
        if part == 0:
            v_at = slice(width + pair * PAIR, width + (pair + 1) * PAIR)
            values = jnp.concatenate([kv_ref[:, v_at], halo[:, v_at]], 0)
            one = jnp.ones_like(values)
            v_ref[pair % 2, :keys, :PAIR] = jnp.where(low_keys, values, one)
            v_ref[pair % 2, keys:, PAIR:] = jnp.where(low_keys, one, values)
        if step + 1 < len(units):
            following = scores_of(*units[step + 1])
        weights = []
        for half in (scores[:, :keys], scores[:, keys:]):
            fold = half[:, :128]
            for c in range(128, keys, 128):
                fold = jnp.maximum(fold, half[:, c : c + 128])
            top = jnp.max(fold, axis=1, keepdims=True)
            weights.append(jnp.exp2((half - top).astype(BF16)))
        mixed = dot(jnp.concatenate(weights, 1), v_ref[pair % 2])
        even, odd = mixed[:, :PAIR], mixed[:, PAIR:]
        total = pltpu.roll(jnp.where(low, odd, even), HEAD_DIM, 1)
        mixed_ref[part * span : (part + 1) * span, pair * PAIR : (pair + 1) * PAIR] = (
            jnp.where(low, even, odd) / total
        ).astype(BF16)
    for copy in copies:
        copy.wait()
    state = nodes_ref[...].astype(F32) + dot(mixed_ref[...], w_out_ref[...])
    state = state.astype(BF16)
    nodes_ref[...] = state
    out = pltpu.make_async_copy(nodes_ref, state_hbm, sent)
    out.start()
    table_ref[...] = dot(state, w_target_ref[...]).astype(BF16)
    out.wait()


def answer(request_ref, table_ref, answer_hbm, answer_ref, sent):
    bricks = request_ref.shape[0]
    capacity = answer_ref.shape[0] // bricks
    columns = jnp.transpose(request_ref[...])
    lanes = iota((capacity, table_ref.shape[0]), 1)
    hot = [ones_where(columns[:capacity, b : b + 1] == lanes) for b in range(bricks)]
    hot = jnp.concatenate(hot, 0)
    half = table_ref.shape[1] // 2
    copies = []
    for part in range(2):
        at = pl.ds(part * half, half)
        answer_ref[:, at] = dot(hot, table_ref[:, at]).astype(BF16)
        copies.append(
            pltpu.make_async_copy(answer_ref.at[:, at], answer_hbm.at[:, at], sent.at[part])
        )
        copies[-1].start()
    for copy in copies:
        copy.wait()


def own_part(
    index_ref, state_ref, w_source_ref, contact_ref, w_ref, part_ref
):
    rows = picked(index_ref[...], state_ref[...]).astype(BF16)
    rows = dot(rows, w_source_ref[...]).astype(BF16).astype(F32)
    part_ref[...] = rows + dot(contact_ref[...], w_ref[...])


def score(place_ref, answers_ref, part_ref, w_ref, out_ref):
    hot = hot_rows(place_ref[...], answers_ref.shape[0])
    half = answers_ref.shape[1] // 2
    folded = jnp.zeros((part_ref.shape[0], 128), F32)
    found = [dot(hot, answers_ref[:, at : at + half]) for at in (0, half)]
    for part in range(2):
        at = slice(part * half, (part + 1) * half)
        weighted = jax.nn.gelu(part_ref[:, at] + found[part]) * w_ref[:, at]
        for c in range(0, half, 128):
            folded = folded + weighted[:, c : c + 128]
    out_ref[...] = jnp.sum(jnp.transpose(folded), axis=0, keepdims=True)


def near(array):
    return pltpu.with_memory_space_constraint(array, pltpu.VMEM)


def away(array):
    return pltpu.with_memory_space_constraint(array, pltpu.HBM)


def run(kernel, outs, *args, scratch=(), mib=16, far=0, far_outs=0):
    space = pl.BlockSpec(memory_space=pltpu.VMEM)
    left = pl.BlockSpec(memory_space=FAR)
    args = [away(arg) for arg in args[:far]] + list(args[far:])
    return pl.pallas_call(
        kernel,
        out_shape=tuple(outs),
        in_specs=[left] * far + [space] * (len(args) - far),
        out_specs=(left,) * far_outs + (space,) * (len(outs) - far_outs),
        scratch_shapes=scratch,
        compiler_params=pltpu.CompilerParams(vmem_limit_bytes=mib * 1024 * 1024),
    )(*args)


def shape(dims, dtype):
    return jax.ShapeDtypeStruct(dims, dtype)


def neighbours(block):
    steps = []
    for axis in ("gy", "gz"):
        count = lax.axis_size(axis)
        for first in range(min(2, count - 1)):
            swaps = []
            for i in range(first, count - 1, 2):
                swaps += [(i, i + 1), (i + 1, i)]
            steps.append((axis, swaps))
    return [lax.ppermute(block, axis, swaps) for axis, swaps in reversed(steps)]


def local(
    nodes,
    block_mask,
    border_ids,
    contact,
    edge_source,
    edge_target,
    edge_owner,
    norm_gain,
    w_qkv,
    w_attn_out,
    w_source,
    w_target,
    w_contact,
    w_score,
):
    rows, width = nodes.shape
    edges = edge_source.shape[0]
    border_count = border_ids.shape[0]
    bricks = lax.axis_size("gy") * lax.axis_size("gz")
    capacity = max(2 * edges // bricks, 2)
    hidden = w_target.shape[1]
    integer = jnp.int32
    border, request, place, nodes_near, gain, mask, w_near = run(
        functools.partial(prepare, dims=(bricks, capacity)),
        (
            shape((border_count + 16, width), BF16),
            shape((bricks, 128), integer),
            shape((edges // 128, 128), integer),
            pltpu.VMEM((rows, width), BF16),
            pltpu.VMEM((1, width), F32),
            pltpu.VMEM(block_mask.shape, integer),
            pltpu.VMEM((width, 3 * width), BF16),
        ),
        border_ids.reshape(border_count // 128, 128),
        edge_owner.reshape(1, edges),
        edge_target.reshape(1, edges),
        nodes,
        norm_gain.reshape(1, width),
        block_mask,
        w_qkv,
        far=7,
        scratch=[
            pltpu.VMEM((border_count // 128, 128), integer),
            pltpu.VMEM((1, edges), integer),
            pltpu.VMEM((1, edges), integer),
            pltpu.SemaphoreType.DMA((7,)),
        ],
    )
    asked = lax.all_to_all(request, ("gy", "gz"), split_axis=0, concat_axis=0, tiled=True)
    halo = neighbours(border)

    q, kv = run(
        project,
        (pltpu.VMEM((rows, width), BF16), pltpu.VMEM((rows, 2 * width), BF16)),
        nodes_near,
        gain,
        w_near,
    )
    keys = rows + len(halo) * border_count
    node_state, table = run(
        functools.partial(attend, pieces=len(halo)),
        (shape((rows, width), BF16), pltpu.VMEM((rows, hidden), BF16)),
        w_attn_out,
        w_target,
        nodes,
        gain,
        mask,
        w_near,
        q,
        kv,
        *[near(piece) for piece in halo],
        far=3,
        mib=40,
        scratch=[
            pltpu.VMEM((width, width), BF16),
            pltpu.VMEM((width, hidden), BF16),
            pltpu.VMEM((rows, width), BF16),
            pltpu.VMEM((rows, width), BF16),
            pltpu.VMEM((2, 2 * keys, 2 * PAIR), BF16),
            pltpu.SemaphoreType.DMA((3,)),
            pltpu.SemaphoreType.DMA,
        ],
        far_outs=1,
    )
    (answers,) = run(
        answer,
        (shape((bricks * capacity, hidden), BF16),),
        near(asked),
        table,
        scratch=[
            pltpu.VMEM((bricks * capacity, hidden), BF16),
            pltpu.SemaphoreType.DMA((2,)),
        ],
        far_outs=1,
    )
    answers = lax.all_to_all(
        answers.reshape(bricks, capacity, hidden),
        ("gy", "gz"),
        split_axis=0,
        concat_axis=0,
        tiled=True,
    ).reshape(bricks * capacity, hidden)
    (part,) = run(
        own_part,
        (pltpu.VMEM((edges, hidden), F32),),
        edge_source.reshape(edges // 128, 128),
        node_state,
        w_source,
        contact,
        w_contact,
    )
    (scores,) = run(
        score, (shape((1, edges), F32),), place, near(answers), part, w_score.reshape(1, hidden)
    )
    return (node_state, scores.reshape(edges))


def solution(mesh):
    split = ("groups", "gy", "gz")
    in_specs = (
        P(split, None),
        P(split, None),
        P(split),
        P(split, None),
        P(split),
        P(split),
        P(split, None),
        P(),
        P(),
        P(),
        P(),
        P(),
        P(),
        P(),
    )
    out_specs = (P(split, None), P(split))
    return jax.shard_map(local, mesh=mesh, in_specs=in_specs, out_specs=out_specs, check_vma=False)
```

```python
import functools

import jax
import jax.numpy as jnp
from jax import lax
from jax.experimental import pallas as pl
from jax.experimental.pallas import tpu as pltpu
from jax.sharding import PartitionSpec as P

HEADS = 8
HEAD_DIM = 64
BLOCK = 128
PAIR = 2 * HEAD_DIM
F32 = jnp.float32
BF16 = jnp.bfloat16
FAR = pltpu.HBM
NT = (((1,), (1,)), ((), ()))


def dot(lhs, rhs):
    return jnp.dot(lhs, rhs, preferred_element_type=F32)


def dot_nt(lhs, rhs):
    return lax.dot_general(lhs, rhs, NT, preferred_element_type=F32)


def ones_where(condition):
    return jnp.where(condition, 1.0, 0.0).astype(BF16)


def iota(shape, axis):
    return lax.broadcasted_iota(jnp.int32, shape, axis)


def columns_of(rows):
    count, lanes = rows.shape
    if count < 8:
        rows = jnp.concatenate([rows] * (8 // count), 0)
    return jnp.transpose(rows)


def hot_rows(index_rows, size):
    count = index_rows.shape[0]
    columns = columns_of(index_rows)
    lanes = iota((128, size), 1)
    return jnp.concatenate([ones_where(columns[:, r : r + 1] == lanes) for r in range(count)], 0)


def picked(index_rows, table):
    return dot(hot_rows(index_rows, table.shape[0]), table)


def normed_rows(values, gain):
    wide = values.astype(F32)
    mean = jnp.mean(wide * wide, axis=-1, keepdims=True)
    return (wide * lax.rsqrt(mean + 1e-06) * gain).astype(BF16)


def fetch(sources, places, signals):
    copies = [
        pltpu.make_async_copy(source, place, signals.at[i])
        for i, (source, place) in enumerate(zip(sources, places))
    ]
    for copy in copies:
        copy.start()
    return copies


def prepare(*refs, dims):
    border_ref, request_ref, place_ref, nodes_ref, gain_ref, mask_ref, w_ref = refs[7:14]
    ids_ref, owner_ref, target_ref, signals = refs[14:]
    places = (ids_ref, owner_ref, target_ref, nodes_ref, gain_ref, mask_ref, w_ref)
    copies = fetch(refs[:7], places, signals)
    for copy in copies[:3]:
        copy.wait()
    bricks, capacity = dims
    edges = owner_ref.shape[1]
    owner = owner_ref[...]
    target = target_ref[...]
    mine = iota((bricks, edges), 0) == owner
    mine_f = jnp.where(mine, 1.0, 0.0)
    before = ones_where(iota((edges, edges), 0) < iota((edges, edges), 1))
    counts = dot(mine_f.astype(BF16), before)
    slots = jnp.sum(counts * mine_f, axis=0, keepdims=True).astype(jnp.int32)
    place = owner * capacity + slots
    for r in range(edges // 128):
        place_ref[r : r + 1, :] = place[:, r * 128 : (r + 1) * 128]
    at_slot = ones_where(iota((128, edges), 0) == slots)
    high = (mine_f * (target >> 5).astype(F32)).astype(BF16)
    low = (mine_f * (target & 31).astype(F32)).astype(BF16)
    request = dot_nt(high, at_slot) * 32.0 + dot_nt(low, at_slot)
    request_ref[...] = request.astype(jnp.int32)
    border = ids_ref.shape[0] * 128
    hot = hot_rows(ids_ref[...], nodes_ref.shape[0])
    copies[3].wait()
    border_ref[:border, :] = dot(hot, nodes_ref[...]).astype(BF16)
    border_ref[border:, :] = jnp.ones_like(border_ref[border:, :])
    for copy in copies[4:]:
        copy.wait()


def project(nodes_ref, gain_ref, w_ref, q_ref, kv_ref):
    width = nodes_ref.shape[1]
    normed = normed_rows(nodes_ref[...], gain_ref[...])
    scale = 1.4426950408889634 / HEAD_DIM**0.5
    q_ref[...] = (dot(normed, w_ref[:, :width]) * scale).astype(BF16)
    kv_ref[...] = dot(normed, w_ref[:, width:]).astype(BF16)


def attend(*refs, pieces):
    w_out_hbm, w_target_hbm, nodes_hbm, gain_ref, mask_ref, w_ref, q_ref, kv_ref = refs[:8]
    halo_refs = refs[8 : 8 + pieces]
    state_hbm, table_ref, w_out_ref, w_target_ref, nodes_ref = refs[8 + pieces : 13 + pieces]
    mixed_ref, v_ref, signals, sent = refs[13 + pieces :]
    copies = fetch(
        (w_out_hbm, w_target_hbm, nodes_hbm), (w_out_ref, w_target_ref, nodes_ref), signals
    )
    rows, width = q_ref.shape
    blocks = rows // BLOCK
    keys = v_ref.shape[1] // 2
    border = (keys - rows) // pieces
    halo_nodes = jnp.concatenate([ref[:border, :] for ref in halo_refs], 0)
    halo = dot(normed_rows(halo_nodes, gain_ref[...]), w_ref[:, width:]).astype(BF16)
    low_keys = iota((keys, PAIR), 1) < HEAD_DIM
    span = rows // 2
    low = iota((span, PAIR), 1) < HEAD_DIM

    lane = iota((blocks, 128), 1)
    row = iota((blocks, 128), 0)
    seen = dot(mask_ref[...].astype(F32).astype(BF16), ones_where(row == lane))
    seen = jnp.where(row == lane, 1.0, seen)
    for h in range(pieces):
        marker = halo_refs[h][border : border + 1, :128].astype(F32)
        seen = jnp.where(lane == blocks + h, marker, seen)
    bias = jnp.where(seen > 0.5, 0.0, -1e30).astype(BF16)
    bias = jnp.concatenate(
        [jnp.broadcast_to(bias[b : b + 1, :], (BLOCK, 128)) for b in range(blocks)], 0
    )
    own = iota((rows, 128), 0) // BLOCK
    far = blocks + iota((keys - rows, 128), 0) // border
    key_block = jnp.concatenate(
        [ones_where(own == iota(own.shape, 1)), ones_where(far == iota(far.shape, 1))], 0
    )
    key_block = jnp.concatenate([key_block, key_block], 0)
    for buffer in range(2):
        v_ref[buffer, :keys, PAIR:] = jnp.zeros((keys, PAIR), BF16)
        v_ref[buffer, keys:, :PAIR] = jnp.zeros((keys, PAIR), BF16)

    def scores_of(pair, part):
        at = slice(pair * PAIR, (pair + 1) * PAIR)
        span_at = slice(part * span, (part + 1) * span)
        k_pair = jnp.concatenate([kv_ref[:, at], halo[:, at]], 0)
        zero = jnp.zeros_like(k_pair)
        k_pair = jnp.concatenate(
            [jnp.where(low_keys, k_pair, zero), jnp.where(low_keys, zero, k_pair)], 0
        )
        k_pair = jnp.concatenate([k_pair, key_block], 1)
        return dot_nt(jnp.concatenate([q_ref[span_at, at], bias[span_at]], 1), k_pair)

    def finish(part):
        at = pl.ds(part * span, span)
        state = nodes_ref[at, :].astype(F32) + dot(mixed_ref[at, :], w_out_ref[...])
        state = state.astype(BF16)
        nodes_ref[at, :] = state
        out = pltpu.make_async_copy(nodes_ref.at[at], state_hbm.at[at], sent.at[part])
        out.start()
        table_ref[at, :] = dot(state, w_target_ref[...]).astype(BF16)
        return out

    outs = []
    units = [(pair, part) for pair in range(width // PAIR) for part in range(2)]
    following = scores_of(*units[0])
    for step, (pair, part) in enumerate(units):
        scores = following
        if part == 0:
            v_at = slice(width + pair * PAIR, width + (pair + 1) * PAIR)
            values = jnp.concatenate([kv_ref[:, v_at], halo[:, v_at]], 0)
            one = jnp.ones_like(values)
            v_ref[pair % 2, :keys, :PAIR] = jnp.where(low_keys, values, one)
            v_ref[pair % 2, keys:, PAIR:] = jnp.where(low_keys, one, values)
        if step + 1 < len(units):
            following = scores_of(*units[step + 1])
        else:
            for copy in copies:
                copy.wait()
            outs.append(finish(0))
        weights = []
        for half in (scores[:, :keys], scores[:, keys:]):
            fold = half[:, :128]
            for c in range(128, keys, 128):
                fold = jnp.maximum(fold, half[:, c : c + 128])
            top = jnp.max(fold, axis=1, keepdims=True)
            weights.append(jnp.exp2((half - top).astype(BF16)))
        mixed = dot(jnp.concatenate(weights, 1), v_ref[pair % 2])
        even, odd = mixed[:, :PAIR], mixed[:, PAIR:]
        total = pltpu.roll(jnp.where(low, odd, even), HEAD_DIM, 1)
        mixed_ref[part * span : (part + 1) * span, pair * PAIR : (pair + 1) * PAIR] = (
            jnp.where(low, even, odd) / total
        ).astype(BF16)
    outs.append(finish(1))
    for out in outs:
        out.wait()


def answer(request_ref, table_ref, answer_hbm, answer_ref, sent):
    bricks = request_ref.shape[0]
    capacity = answer_ref.shape[0] // bricks
    columns = jnp.transpose(request_ref[...])
    lanes = iota((capacity, table_ref.shape[0]), 1)
    copies = []
    for first in range(0, bricks, bricks // 4):
        hot = [
            ones_where(columns[:capacity, b : b + 1] == lanes)
            for b in range(first, first + bricks // 4)
        ]
        at = pl.ds(first * capacity, bricks // 4 * capacity)
        answer_ref[at, :] = dot(jnp.concatenate(hot, 0), table_ref[...]).astype(BF16)
        copies.append(
            pltpu.make_async_copy(
                answer_ref.at[at], answer_hbm.at[at], sent.at[first // (bricks // 4)]
            )
        )
        copies[-1].start()
    for copy in copies:
        copy.wait()


def own_part(
    index_ref, state_ref, w_source_ref, contact_ref, w_ref, part_ref
):
    rows = picked(index_ref[...], state_ref[...]).astype(BF16)
    rows = dot(rows, w_source_ref[...]).astype(BF16).astype(F32)
    part_ref[...] = rows + dot(contact_ref[...], w_ref[...])


def score(place_ref, answers_ref, part_ref, w_ref, out_ref):
    pre = part_ref[...] + picked(place_ref[...], answers_ref[...])
    weighted = jax.nn.gelu(pre) * w_ref[...]
    folded = weighted[:, :128]
    for at in range(128, weighted.shape[1], 128):
        folded = folded + weighted[:, at : at + 128]
    out_ref[...] = jnp.sum(jnp.transpose(folded), axis=0, keepdims=True)


def near(array):
    return pltpu.with_memory_space_constraint(array, pltpu.VMEM)


def away(array):
    return pltpu.with_memory_space_constraint(array, pltpu.HBM)


def run(kernel, outs, *args, scratch=(), mib=16, far=0, far_outs=0):
    space = pl.BlockSpec(memory_space=pltpu.VMEM)
    left = pl.BlockSpec(memory_space=FAR)
    args = [away(arg) for arg in args[:far]] + list(args[far:])
    return pl.pallas_call(
        kernel,
        out_shape=tuple(outs),
        in_specs=[left] * far + [space] * (len(args) - far),
        out_specs=(left,) * far_outs + (space,) * (len(outs) - far_outs),
        scratch_shapes=scratch,
        compiler_params=pltpu.CompilerParams(vmem_limit_bytes=mib * 1024 * 1024),
    )(*args)


def shape(dims, dtype):
    return jax.ShapeDtypeStruct(dims, dtype)


def neighbours(block):
    steps = []
    for axis in ("gy", "gz"):
        count = lax.axis_size(axis)
        for first in range(min(2, count - 1)):
            swaps = []
            for i in range(first, count - 1, 2):
                swaps += [(i, i + 1), (i + 1, i)]
            steps.append((axis, swaps))
    return [lax.ppermute(block, axis, swaps) for axis, swaps in reversed(steps)]


def local(
    nodes,
    block_mask,
    border_ids,
    contact,
    edge_source,
    edge_target,
    edge_owner,
    norm_gain,
    w_qkv,
    w_attn_out,
    w_source,
    w_target,
    w_contact,
    w_score,
):
    rows, width = nodes.shape
    edges = edge_source.shape[0]
    border_count = border_ids.shape[0]
    bricks = lax.axis_size("gy") * lax.axis_size("gz")
    capacity = max(2 * edges // bricks, 2)
    hidden = w_target.shape[1]
    integer = jnp.int32
    border, request, place, nodes_near, gain, mask, w_near = run(
        functools.partial(prepare, dims=(bricks, capacity)),
        (
            shape((border_count + 16, width), BF16),
            shape((bricks, 128), integer),
            shape((edges // 128, 128), integer),
            pltpu.VMEM((rows, width), BF16),
            pltpu.VMEM((1, width), F32),
            pltpu.VMEM(block_mask.shape, integer),
            pltpu.VMEM((width, 3 * width), BF16),
        ),
        border_ids.reshape(border_count // 128, 128),
        edge_owner.reshape(1, edges),
        edge_target.reshape(1, edges),
        nodes,
        norm_gain.reshape(1, width),
        block_mask,
        w_qkv,
        far=7,
        scratch=[
            pltpu.VMEM((border_count // 128, 128), integer),
            pltpu.VMEM((1, edges), integer),
            pltpu.VMEM((1, edges), integer),
            pltpu.SemaphoreType.DMA((7,)),
        ],
    )
    asked = lax.all_to_all(request, ("gy", "gz"), split_axis=0, concat_axis=0, tiled=True)
    halo = neighbours(border)

    q, kv = run(
        project,
        (pltpu.VMEM((rows, width), BF16), pltpu.VMEM((rows, 2 * width), BF16)),
        nodes_near,
        gain,
        w_near,
    )
    keys = rows + len(halo) * border_count
    node_state, table = run(
        functools.partial(attend, pieces=len(halo)),
        (shape((rows, width), BF16), pltpu.VMEM((rows, hidden), BF16)),
        w_attn_out,
        w_target,
        nodes,
        gain,
        mask,
        w_near,
        q,
        kv,
        *[near(piece) for piece in halo],
        far=3,
        mib=40,
        scratch=[
            pltpu.VMEM((width, width), BF16),
            pltpu.VMEM((width, hidden), BF16),
            pltpu.VMEM((rows, width), BF16),
            pltpu.VMEM((rows, width), BF16),
            pltpu.VMEM((2, 2 * keys, 2 * PAIR), BF16),
            pltpu.SemaphoreType.DMA((3,)),
            pltpu.SemaphoreType.DMA((2,)),
        ],
        far_outs=1,
    )
    (answers,) = run(
        answer,
        (shape((bricks * capacity, hidden), BF16),),
        near(asked),
        table,
        scratch=[
            pltpu.VMEM((bricks * capacity, hidden), BF16),
            pltpu.SemaphoreType.DMA((4,)),
        ],
        far_outs=1,
    )
    answers = lax.all_to_all(
        answers.reshape(bricks, capacity, hidden),
        ("gy", "gz"),
        split_axis=0,
        concat_axis=0,
        tiled=True,
    ).reshape(bricks * capacity, hidden)
    (part,) = run(
        own_part,
        (pltpu.VMEM((edges, hidden), F32),),
        edge_source.reshape(edges // 128, 128),
        node_state,
        w_source,
        contact,
        w_contact,
    )
    (scores,) = run(
        score, (shape((1, edges), F32),), place, near(answers), part, w_score.reshape(1, hidden)
    )
    return (node_state, scores.reshape(edges))


def solution(mesh):
    split = ("groups", "gy", "gz")
    in_specs = (
        P(split, None),
        P(split, None),
        P(split),
        P(split, None),
        P(split),
        P(split),
        P(split, None),
        P(),
        P(),
        P(),
        P(),
        P(),
        P(),
        P(),
    )
    out_specs = (P(split, None), P(split))
    return jax.shard_map(local, mesh=mesh, in_specs=in_specs, out_specs=out_specs, check_vma=False)
```

```python
import functools

import jax
import jax.numpy as jnp
from jax import lax
from jax.experimental import pallas as pl
from jax.experimental.pallas import tpu as pltpu
from jax.sharding import PartitionSpec as P

HEADS = 8
HEAD_DIM = 64
BLOCK = 128
PAIR = 2 * HEAD_DIM
F32 = jnp.float32
BF16 = jnp.bfloat16
FAR = pltpu.HBM
NT = (((1,), (1,)), ((), ()))


def dot(lhs, rhs):
    return jnp.dot(lhs, rhs, preferred_element_type=F32)


def dot_nt(lhs, rhs):
    return lax.dot_general(lhs, rhs, NT, preferred_element_type=F32)


def ones_where(condition):
    return jnp.where(condition, 1.0, 0.0).astype(BF16)


def iota(shape, axis):
    return lax.broadcasted_iota(jnp.int32, shape, axis)


def columns_of(rows):
    count, lanes = rows.shape
    if count < 8:
        rows = jnp.concatenate([rows] * (8 // count), 0)
    return jnp.transpose(rows)


def hot_rows(index_rows, size):
    count = index_rows.shape[0]
    columns = columns_of(index_rows)
    lanes = iota((128, size), 1)
    return jnp.concatenate([ones_where(columns[:, r : r + 1] == lanes) for r in range(count)], 0)


def picked(index_rows, table):
    return dot(hot_rows(index_rows, table.shape[0]), table)


def normed_rows(values, gain):
    wide = values.astype(F32)
    mean = jnp.mean(wide * wide, axis=-1, keepdims=True)
    return (wide * lax.rsqrt(mean + 1e-06) * gain).astype(BF16)


def fetch(sources, places, signals):
    copies = [
        pltpu.make_async_copy(source, place, signals.at[i])
        for i, (source, place) in enumerate(zip(sources, places))
    ]
    for copy in copies:
        copy.start()
    return copies


def prepare(*refs, dims):
    border_ref, request_ref, place_ref, nodes_ref, gain_ref, mask_ref, w_ref = refs[7:14]
    ids_ref, owner_ref, target_ref, signals = refs[14:]
    places = (ids_ref, owner_ref, target_ref, nodes_ref, gain_ref, mask_ref, w_ref)
    copies = fetch(refs[:7], places, signals)
    for copy in copies[:3]:
        copy.wait()
    bricks, capacity = dims
    edges = owner_ref.shape[1]
    owner = owner_ref[...]
    target = target_ref[...]
    mine = iota((bricks, edges), 0) == owner
    mine_f = jnp.where(mine, 1.0, 0.0)
    before = ones_where(iota((edges, edges), 0) < iota((edges, edges), 1))
    counts = dot(mine_f.astype(BF16), before)
    slots = jnp.sum(counts * mine_f, axis=0, keepdims=True).astype(jnp.int32)
    place = owner * capacity + slots
    for r in range(edges // 128):
        place_ref[r : r + 1, :] = place[:, r * 128 : (r + 1) * 128]
    at_slot = ones_where(iota((128, edges), 0) == slots)
    high = (mine_f * (target >> 5).astype(F32)).astype(BF16)
    low = (mine_f * (target & 31).astype(F32)).astype(BF16)
    request = dot_nt(high, at_slot) * 32.0 + dot_nt(low, at_slot)
    request_ref[...] = request.astype(jnp.int32)
    border = ids_ref.shape[0] * 128
    hot = hot_rows(ids_ref[...], nodes_ref.shape[0])
    copies[3].wait()
    border_ref[:border, :] = dot(hot, nodes_ref[...]).astype(BF16)
    border_ref[border:, :] = jnp.ones_like(border_ref[border:, :])
    for copy in copies[4:]:
        copy.wait()


def project(nodes_ref, gain_ref, w_ref, q_ref, kv_ref):
    width = nodes_ref.shape[1]
    normed = normed_rows(nodes_ref[...], gain_ref[...])
    scale = 1.4426950408889634 / HEAD_DIM**0.5
    q_ref[...] = (dot(normed, w_ref[:, :width]) * scale).astype(BF16)
    kv_ref[...] = dot(normed, w_ref[:, width:]).astype(BF16)


def attend(*refs, pieces):
    w_out_hbm, w_target_hbm, nodes_hbm, gain_ref, mask_ref, w_ref, q_ref, kv_ref = refs[:8]
    halo_refs = refs[8 : 8 + pieces]
    state_hbm, table_ref, w_out_ref, w_target_ref, nodes_ref = refs[8 + pieces : 13 + pieces]
    mixed_ref, v_ref, signals, sent = refs[13 + pieces :]
    copies = fetch(
        (w_out_hbm, w_target_hbm, nodes_hbm), (w_out_ref, w_target_ref, nodes_ref), signals
    )
    rows, width = q_ref.shape
    blocks = rows // BLOCK
    keys = v_ref.shape[1] // 2
    border = (keys - rows) // pieces
    halo_nodes = jnp.concatenate([ref[:border, :] for ref in halo_refs], 0)
    halo = dot(normed_rows(halo_nodes, gain_ref[...]), w_ref[:, width:]).astype(BF16)
    low_keys = iota((keys, PAIR), 1) < HEAD_DIM
    span = rows // 2
    low = iota((span, PAIR), 1) < HEAD_DIM

    lane = iota((blocks, 128), 1)
    row = iota((blocks, 128), 0)
    seen = dot(mask_ref[...].astype(F32).astype(BF16), ones_where(row == lane))
    seen = jnp.where(row == lane, 1.0, seen)
    for h in range(pieces):
        marker = halo_refs[h][border : border + 1, :128].astype(F32)
        seen = jnp.where(lane == blocks + h, marker, seen)
    bias = jnp.where(seen > 0.5, 0.0, -1e30).astype(BF16)
    bias = jnp.concatenate(
        [jnp.broadcast_to(bias[b : b + 1, :], (BLOCK, 128)) for b in range(blocks)], 0
    )
    own = iota((rows, 128), 0) // BLOCK
    far = blocks + iota((keys - rows, 128), 0) // border
    key_block = jnp.concatenate(
        [ones_where(own == iota(own.shape, 1)), ones_where(far == iota(far.shape, 1))], 0
    )
    key_block = jnp.concatenate([key_block, key_block], 0)
    for buffer in range(2):
        v_ref[buffer, :keys, PAIR:] = jnp.zeros((keys, PAIR), BF16)
        v_ref[buffer, keys:, :PAIR] = jnp.zeros((keys, PAIR), BF16)

    def scores_of(pair, part):
        at = slice(pair * PAIR, (pair + 1) * PAIR)
        span_at = slice(part * span, (part + 1) * span)
        k_pair = jnp.concatenate([kv_ref[:, at], halo[:, at]], 0)
        zero = jnp.zeros_like(k_pair)
        k_pair = jnp.concatenate(
            [jnp.where(low_keys, k_pair, zero), jnp.where(low_keys, zero, k_pair)], 0
        )
        k_pair = jnp.concatenate([k_pair, key_block], 1)
        return dot_nt(jnp.concatenate([q_ref[span_at, at], bias[span_at]], 1), k_pair)

    copies[0].wait()
    copies[1].wait()
    units = [(pair, part) for pair in range(width // PAIR) for part in range(2)]
    following = scores_of(*units[0])
    for step, (pair, part) in enumerate(units):
        scores = following
        if part == 0:
            v_at = slice(width + pair * PAIR, width + (pair + 1) * PAIR)
            values = jnp.concatenate([kv_ref[:, v_at], halo[:, v_at]], 0)
            one = jnp.ones_like(values)
            v_ref[pair % 2, :keys, :PAIR] = jnp.where(low_keys, values, one)
            v_ref[pair % 2, keys:, PAIR:] = jnp.where(low_keys, one, values)
        if step + 1 < len(units):
            following = scores_of(*units[step + 1])
        weights = []
        for half in (scores[:, :keys], scores[:, keys:]):
            fold = half[:, :128]
            for c in range(128, keys, 128):
                fold = jnp.maximum(fold, half[:, c : c + 128])
            top = jnp.max(fold, axis=1, keepdims=True)
            weights.append(jnp.exp2((half - top).astype(BF16)))
        mixed = dot(jnp.concatenate(weights, 1), v_ref[pair % 2])
        even, odd = mixed[:, :PAIR], mixed[:, PAIR:]
        total = pltpu.roll(jnp.where(low, odd, even), HEAD_DIM, 1)
        mixed_ref[part * span : (part + 1) * span, pair * PAIR : (pair + 1) * PAIR] = (
            jnp.where(low, even, odd) / total
        ).astype(BF16)
    update = dot(mixed_ref[...], w_out_ref[...])
    copies[2].wait()
    state = nodes_ref[...].astype(F32) + update
    state = state.astype(BF16)
    nodes_ref[...] = state
    out = pltpu.make_async_copy(nodes_ref, state_hbm, sent)
    out.start()
    table_ref[...] = dot(state, w_target_ref[...]).astype(BF16)
    out.wait()


def answer(request_ref, table_ref, answer_hbm, answer_ref, sent):
    bricks = request_ref.shape[0]
    capacity = answer_ref.shape[0] // bricks
    columns = jnp.transpose(request_ref[...])
    lanes = iota((capacity, table_ref.shape[0]), 1)
    copies = []
    for first in range(0, bricks, bricks // 4):
        hot = [
            ones_where(columns[:capacity, b : b + 1] == lanes)
            for b in range(first, first + bricks // 4)
        ]
        at = pl.ds(first * capacity, bricks // 4 * capacity)
        answer_ref[at, :] = dot(jnp.concatenate(hot, 0), table_ref[...]).astype(BF16)
        copies.append(
            pltpu.make_async_copy(
                answer_ref.at[at], answer_hbm.at[at], sent.at[first // (bricks // 4)]
            )
        )
        copies[-1].start()
    for copy in copies:
        copy.wait()


def own_part(
    index_ref, state_ref, w_source_ref, contact_ref, w_ref, part_ref
):
    rows = picked(index_ref[...], state_ref[...]).astype(BF16)
    rows = dot(rows, w_source_ref[...]).astype(BF16).astype(F32)
    part_ref[...] = rows + dot(contact_ref[...], w_ref[...])


def score(place_ref, answers_ref, part_ref, w_ref, out_ref):
    pre = part_ref[...] + picked(place_ref[...], answers_ref[...])
    weighted = jax.nn.gelu(pre) * w_ref[...]
    folded = weighted[:, :128]
    for at in range(128, weighted.shape[1], 128):
        folded = folded + weighted[:, at : at + 128]
    out_ref[...] = jnp.sum(jnp.transpose(folded), axis=0, keepdims=True)


def near(array):
    return pltpu.with_memory_space_constraint(array, pltpu.VMEM)


def away(array):
    return pltpu.with_memory_space_constraint(array, pltpu.HBM)


def run(kernel, outs, *args, scratch=(), mib=16, far=0, far_outs=0):
    space = pl.BlockSpec(memory_space=pltpu.VMEM)
    left = pl.BlockSpec(memory_space=FAR)
    args = [away(arg) for arg in args[:far]] + list(args[far:])
    return pl.pallas_call(
        kernel,
        out_shape=tuple(outs),
        in_specs=[left] * far + [space] * (len(args) - far),
        out_specs=(left,) * far_outs + (space,) * (len(outs) - far_outs),
        scratch_shapes=scratch,
        compiler_params=pltpu.CompilerParams(vmem_limit_bytes=mib * 1024 * 1024),
    )(*args)


def shape(dims, dtype):
    return jax.ShapeDtypeStruct(dims, dtype)


def neighbours(block):
    steps = []
    for axis in ("gy", "gz"):
        count = lax.axis_size(axis)
        for first in range(min(2, count - 1)):
            swaps = []
            for i in range(first, count - 1, 2):
                swaps += [(i, i + 1), (i + 1, i)]
            steps.append((axis, swaps))
    return [lax.ppermute(block, axis, swaps) for axis, swaps in reversed(steps)]


def local(
    nodes,
    block_mask,
    border_ids,
    contact,
    edge_source,
    edge_target,
    edge_owner,
    norm_gain,
    w_qkv,
    w_attn_out,
    w_source,
    w_target,
    w_contact,
    w_score,
):
    rows, width = nodes.shape
    edges = edge_source.shape[0]
    border_count = border_ids.shape[0]
    bricks = lax.axis_size("gy") * lax.axis_size("gz")
    capacity = max(2 * edges // bricks, 2)
    hidden = w_target.shape[1]
    integer = jnp.int32
    border, request, place, nodes_near, gain, mask, w_near = run(
        functools.partial(prepare, dims=(bricks, capacity)),
        (
            shape((border_count + 16, width), BF16),
            shape((bricks, 128), integer),
            shape((edges // 128, 128), integer),
            pltpu.VMEM((rows, width), BF16),
            pltpu.VMEM((1, width), F32),
            pltpu.VMEM(block_mask.shape, integer),
            pltpu.VMEM((width, 3 * width), BF16),
        ),
        border_ids.reshape(border_count // 128, 128),
        edge_owner.reshape(1, edges),
        edge_target.reshape(1, edges),
        nodes,
        norm_gain.reshape(1, width),
        block_mask,
        w_qkv,
        far=7,
        scratch=[
            pltpu.VMEM((border_count // 128, 128), integer),
            pltpu.VMEM((1, edges), integer),
            pltpu.VMEM((1, edges), integer),
            pltpu.SemaphoreType.DMA((7,)),
        ],
    )
    asked = lax.all_to_all(request, ("gy", "gz"), split_axis=0, concat_axis=0, tiled=True)
    halo = neighbours(border)

    q, kv = run(
        project,
        (pltpu.VMEM((rows, width), BF16), pltpu.VMEM((rows, 2 * width), BF16)),
        nodes_near,
        gain,
        w_near,
    )
    keys = rows + len(halo) * border_count
    node_state, table = run(
        functools.partial(attend, pieces=len(halo)),
        (shape((rows, width), BF16), pltpu.VMEM((rows, hidden), BF16)),
        w_attn_out,
        w_target,
        nodes,
        gain,
        mask,
        w_near,
        q,
        kv,
        *[near(piece) for piece in halo],
        far=3,
        mib=40,
        scratch=[
            pltpu.VMEM((width, width), BF16),
            pltpu.VMEM((width, hidden), BF16),
            pltpu.VMEM((rows, width), BF16),
            pltpu.VMEM((rows, width), BF16),
            pltpu.VMEM((2, 2 * keys, 2 * PAIR), BF16),
            pltpu.SemaphoreType.DMA((3,)),
            pltpu.SemaphoreType.DMA,
        ],
        far_outs=1,
    )
    (answers,) = run(
        answer,
        (shape((bricks * capacity, hidden), BF16),),
        near(asked),
        table,
        scratch=[
            pltpu.VMEM((bricks * capacity, hidden), BF16),
            pltpu.SemaphoreType.DMA((4,)),
        ],
        far_outs=1,
    )
    answers = lax.all_to_all(
        answers.reshape(bricks, capacity, hidden),
        ("gy", "gz"),
        split_axis=0,
        concat_axis=0,
        tiled=True,
    ).reshape(bricks * capacity, hidden)
    (part,) = run(
        own_part,
        (pltpu.VMEM((edges, hidden), F32),),
        edge_source.reshape(edges // 128, 128),
        node_state,
        w_source,
        contact,
        w_contact,
    )
    (scores,) = run(
        score, (shape((1, edges), F32),), place, near(answers), part, w_score.reshape(1, hidden)
    )
    return (node_state, scores.reshape(edges))


def solution(mesh):
    split = ("groups", "gy", "gz")
    in_specs = (
        P(split, None),
        P(split, None),
        P(split),
        P(split, None),
        P(split),
        P(split),
        P(split, None),
        P(),
        P(),
        P(),
        P(),
        P(),
        P(),
        P(),
    )
    out_specs = (P(split, None), P(split))
    return jax.shard_map(local, mesh=mesh, in_specs=in_specs, out_specs=out_specs, check_vma=False)
```

```python
import functools

import jax
import jax.numpy as jnp
from jax import lax
from jax.experimental import pallas as pl
from jax.experimental.pallas import tpu as pltpu
from jax.sharding import PartitionSpec as P

HEADS = 8
HEAD_DIM = 64
BLOCK = 128
PAIR = 2 * HEAD_DIM
F32 = jnp.float32
BF16 = jnp.bfloat16
FAR = pltpu.HBM
NT = (((1,), (1,)), ((), ()))


def dot(lhs, rhs):
    return jnp.dot(lhs, rhs, preferred_element_type=F32)


def dot_nt(lhs, rhs):
    return lax.dot_general(lhs, rhs, NT, preferred_element_type=F32)


def ones_where(condition):
    return jnp.where(condition, 1.0, 0.0).astype(BF16)


def iota(shape, axis):
    return lax.broadcasted_iota(jnp.int32, shape, axis)


def columns_of(rows):
    count, lanes = rows.shape
    if count < 8:
        rows = jnp.concatenate([rows] * (8 // count), 0)
    return jnp.transpose(rows)


def hot_rows(index_rows, size):
    count = index_rows.shape[0]
    columns = columns_of(index_rows)
    lanes = iota((128, size), 1)
    return jnp.concatenate([ones_where(columns[:, r : r + 1] == lanes) for r in range(count)], 0)


def picked(index_rows, table):
    return dot(hot_rows(index_rows, table.shape[0]), table)


def normed_rows(values, gain):
    wide = values.astype(F32)
    mean = jnp.mean(wide * wide, axis=-1, keepdims=True)
    return (wide * lax.rsqrt(mean + 1e-06) * gain).astype(BF16)


def fetch(sources, places, signals):
    copies = [
        pltpu.make_async_copy(source, place, signals.at[i])
        for i, (source, place) in enumerate(zip(sources, places))
    ]
    for copy in copies:
        copy.start()
    return copies


def prepare(*refs, dims):
    border_ref, request_ref, place_ref, nodes_ref, gain_ref, mask_ref, w_ref = refs[7:14]
    ids_ref, owner_ref, target_ref, signals = refs[14:]
    places = (ids_ref, owner_ref, target_ref, nodes_ref, gain_ref, mask_ref, w_ref)
    copies = fetch(refs[:7], places, signals)
    for copy in copies[:3]:
        copy.wait()
    bricks, capacity = dims
    edges = owner_ref.shape[1]
    owner = owner_ref[...]
    target = target_ref[...]
    mine = iota((bricks, edges), 0) == owner
    mine_f = jnp.where(mine, 1.0, 0.0)
    before = ones_where(iota((edges, edges), 0) < iota((edges, edges), 1))
    counts = dot(mine_f.astype(BF16), before)
    slots = jnp.sum(counts * mine_f, axis=0, keepdims=True).astype(jnp.int32)
    place = owner * capacity + slots
    for r in range(edges // 128):
        place_ref[r : r + 1, :] = place[:, r * 128 : (r + 1) * 128]
    at_slot = ones_where(iota((128, edges), 0) == slots)
    high = (mine_f * (target >> 5).astype(F32)).astype(BF16)
    low = (mine_f * (target & 31).astype(F32)).astype(BF16)
    request = dot_nt(high, at_slot) * 32.0 + dot_nt(low, at_slot)
    request_ref[...] = request.astype(jnp.int32)
    border = ids_ref.shape[0] * 128
    hot = hot_rows(ids_ref[...], nodes_ref.shape[0])
    copies[3].wait()
    border_ref[:border, :] = dot(hot, nodes_ref[...]).astype(BF16)
    border_ref[border:, :] = jnp.ones_like(border_ref[border:, :])
    for copy in copies[4:]:
        copy.wait()


def project(nodes_ref, gain_ref, w_ref, q_ref, kv_ref):
    width = nodes_ref.shape[1]
    normed = normed_rows(nodes_ref[...], gain_ref[...])
    scale = 1.4426950408889634 / HEAD_DIM**0.5
    q_ref[...] = (dot(normed, w_ref[:, :width]) * scale).astype(BF16)
    kv_ref[...] = dot(normed, w_ref[:, width:]).astype(BF16)


def attend(*refs, pieces):
    w_out_hbm, w_target_hbm, nodes_hbm, gain_ref, mask_ref, w_ref, q_ref, kv_ref = refs[:8]
    halo_refs = refs[8 : 8 + pieces]
    state_hbm, table_ref, w_out_ref, w_target_ref, nodes_ref = refs[8 + pieces : 13 + pieces]
    mixed_ref, v_ref, signals, sent = refs[13 + pieces :]
    copies = fetch(
        (w_out_hbm, w_target_hbm, nodes_hbm), (w_out_ref, w_target_ref, nodes_ref), signals
    )
    rows, width = q_ref.shape
    blocks = rows // BLOCK
    keys = v_ref.shape[1] // 2
    border = (keys - rows) // pieces
    halo_nodes = jnp.concatenate([ref[:border, :] for ref in halo_refs], 0)
    halo = dot(normed_rows(halo_nodes, gain_ref[...]), w_ref[:, width:]).astype(BF16)
    low_keys = iota((keys, PAIR), 1) < HEAD_DIM
    span = rows // 2
    low = iota((span, PAIR), 1) < HEAD_DIM

    lane = iota((blocks, 128), 1)
    row = iota((blocks, 128), 0)
    seen = dot(mask_ref[...].astype(F32).astype(BF16), ones_where(row == lane))
    seen = jnp.where(row == lane, 1.0, seen)
    for h in range(pieces):
        marker = halo_refs[h][border : border + 1, :128].astype(F32)
        seen = jnp.where(lane == blocks + h, marker, seen)
    bias = jnp.where(seen > 0.5, 0.0, -1e30).astype(BF16)
    bias = jnp.concatenate(
        [jnp.broadcast_to(bias[b : b + 1, :], (BLOCK, 128)) for b in range(blocks)], 0
    )
    own = iota((rows, 128), 0) // BLOCK
    far = blocks + iota((keys - rows, 128), 0) // border
    key_block = jnp.concatenate(
        [ones_where(own == iota(own.shape, 1)), ones_where(far == iota(far.shape, 1))], 0
    )
    key_block = jnp.concatenate([key_block, key_block], 0)
    for buffer in range(2):
        v_ref[buffer, :keys, PAIR:] = jnp.zeros((keys, PAIR), BF16)
        v_ref[buffer, keys:, :PAIR] = jnp.zeros((keys, PAIR), BF16)

    def scores_of(pair, part):
        at = slice(pair * PAIR, (pair + 1) * PAIR)
        span_at = slice(part * span, (part + 1) * span)
        k_pair = jnp.concatenate([kv_ref[:, at], halo[:, at]], 0)
        zero = jnp.zeros_like(k_pair)
        k_pair = jnp.concatenate(
            [jnp.where(low_keys, k_pair, zero), jnp.where(low_keys, zero, k_pair)], 0
        )
        k_pair = jnp.concatenate([k_pair, key_block], 1)
        return dot_nt(jnp.concatenate([q_ref[span_at, at], bias[span_at]], 1), k_pair)

    units = [(pair, part) for pair in range(width // PAIR) for part in range(2)]
    following = scores_of(*units[0])
    for step, (pair, part) in enumerate(units):
        scores = following
        if part == 0:
            v_at = slice(width + pair * PAIR, width + (pair + 1) * PAIR)
            values = jnp.concatenate([kv_ref[:, v_at], halo[:, v_at]], 0)
            one = jnp.ones_like(values)
            v_ref[pair % 2, :keys, :PAIR] = jnp.where(low_keys, values, one)
            v_ref[pair % 2, keys:, PAIR:] = jnp.where(low_keys, one, values)
        if step + 1 < len(units):
            following = scores_of(*units[step + 1])
        weights = []
        for half in (scores[:, :keys], scores[:, keys:]):
            fold = half[:, :128]
            for c in range(128, keys, 128):
                fold = jnp.maximum(fold, half[:, c : c + 128])
            top = jnp.max(fold, axis=1, keepdims=True)
            weights.append(jnp.exp2((half - top).astype(BF16)))
        mixed = dot(jnp.concatenate(weights, 1), v_ref[pair % 2])
        even, odd = mixed[:, :PAIR], mixed[:, PAIR:]
        total = pltpu.roll(jnp.where(low, odd, even), HEAD_DIM, 1)
        mixed_ref[part * span : (part + 1) * span, pair * PAIR : (pair + 1) * PAIR] = (
            jnp.where(low, even, odd) / total
        ).astype(BF16)
    for copy in copies:
        copy.wait()
    state = nodes_ref[...].astype(F32) + dot(mixed_ref[...], w_out_ref[...])
    state = state.astype(BF16)
    nodes_ref[...] = state
    out = pltpu.make_async_copy(nodes_ref, state_hbm, sent)
    out.start()
    table_ref[...] = dot(state, w_target_ref[...]).astype(BF16)
    out.wait()


def answer(request_ref, table_ref, answer_hbm, answer_ref, sent):
    bricks = request_ref.shape[0]
    capacity = answer_ref.shape[0] // bricks
    columns = jnp.transpose(request_ref[...])
    lanes = iota((capacity, table_ref.shape[0]), 1)
    copies = []
    for first in range(0, bricks, bricks // 2):
        hot = [
            ones_where(columns[:capacity, b : b + 1] == lanes)
            for b in range(first, first + bricks // 2)
        ]
        at = pl.ds(first * capacity, bricks // 2 * capacity)
        answer_ref[at, :] = dot(jnp.concatenate(hot, 0), table_ref[...]).astype(BF16)
        copies.append(
            pltpu.make_async_copy(
                answer_ref.at[at], answer_hbm.at[at], sent.at[first // (bricks // 2)]
            )
        )
        copies[-1].start()
    for copy in copies:
        copy.wait()


def own_part(
    index_ref, state_ref, w_source_ref, contact_ref, w_ref, part_ref
):
    rows = picked(index_ref[...], state_ref[...]).astype(BF16)
    rows = dot(rows, w_source_ref[...]).astype(BF16).astype(F32)
    part_ref[...] = rows + dot(contact_ref[...], w_ref[...])


def score(place_ref, answers_ref, part_ref, w_ref, out_ref):
    pre = part_ref[...] + picked(place_ref[...], answers_ref[...])
    weighted = jax.nn.gelu(pre) * w_ref[...]
    folded = weighted[:, :128]
    for at in range(128, weighted.shape[1], 128):
        folded = folded + weighted[:, at : at + 128]
    out_ref[...] = jnp.sum(jnp.transpose(folded), axis=0, keepdims=True)


def near(array):
    return pltpu.with_memory_space_constraint(array, pltpu.VMEM)


def away(array):
    return pltpu.with_memory_space_constraint(array, pltpu.HBM)


def run(kernel, outs, *args, scratch=(), mib=16, far=0, far_outs=0):
    space = pl.BlockSpec(memory_space=pltpu.VMEM)
    left = pl.BlockSpec(memory_space=FAR)
    args = [away(arg) for arg in args[:far]] + list(args[far:])
    return pl.pallas_call(
        kernel,
        out_shape=tuple(outs),
        in_specs=[left] * far + [space] * (len(args) - far),
        out_specs=(left,) * far_outs + (space,) * (len(outs) - far_outs),
        scratch_shapes=scratch,
        compiler_params=pltpu.CompilerParams(vmem_limit_bytes=mib * 1024 * 1024),
    )(*args)


def shape(dims, dtype):
    return jax.ShapeDtypeStruct(dims, dtype)


def neighbours(block):
    steps = []
    for axis in ("gy", "gz"):
        count = lax.axis_size(axis)
        for first in range(min(2, count - 1)):
            swaps = []
            for i in range(first, count - 1, 2):
                swaps += [(i, i + 1), (i + 1, i)]
            steps.append((axis, swaps))
    return [lax.ppermute(block, axis, swaps) for axis, swaps in reversed(steps)]


def local(
    nodes,
    block_mask,
    border_ids,
    contact,
    edge_source,
    edge_target,
    edge_owner,
    norm_gain,
    w_qkv,
    w_attn_out,
    w_source,
    w_target,
    w_contact,
    w_score,
):
    rows, width = nodes.shape
    edges = edge_source.shape[0]
    border_count = border_ids.shape[0]
    bricks = lax.axis_size("gy") * lax.axis_size("gz")
    capacity = max(2 * edges // bricks, 2)
    hidden = w_target.shape[1]
    integer = jnp.int32
    border, request, place, nodes_near, gain, mask, w_near = run(
        functools.partial(prepare, dims=(bricks, capacity)),
        (
            shape((border_count + 16, width), BF16),
            shape((bricks, 128), integer),
            shape((edges // 128, 128), integer),
            pltpu.VMEM((rows, width), BF16),
            pltpu.VMEM((1, width), F32),
            pltpu.VMEM(block_mask.shape, integer),
            pltpu.VMEM((width, 3 * width), BF16),
        ),
        border_ids.reshape(border_count // 128, 128),
        edge_owner.reshape(1, edges),
        edge_target.reshape(1, edges),
        nodes,
        norm_gain.reshape(1, width),
        block_mask,
        w_qkv,
        far=7,
        scratch=[
            pltpu.VMEM((border_count // 128, 128), integer),
            pltpu.VMEM((1, edges), integer),
            pltpu.VMEM((1, edges), integer),
            pltpu.SemaphoreType.DMA((7,)),
        ],
    )
    asked = lax.all_to_all(request, ("gy", "gz"), split_axis=0, concat_axis=0, tiled=True)
    halo = neighbours(border)

    q, kv = run(
        project,
        (pltpu.VMEM((rows, width), BF16), pltpu.VMEM((rows, 2 * width), BF16)),
        nodes_near,
        gain,
        w_near,
    )
    keys = rows + len(halo) * border_count
    node_state, table = run(
        functools.partial(attend, pieces=len(halo)),
        (shape((rows, width), BF16), pltpu.VMEM((rows, hidden), BF16)),
        w_attn_out,
        w_target,
        nodes,
        gain,
        mask,
        w_near,
        q,
        kv,
        *[near(piece) for piece in halo],
        far=3,
        mib=40,
        scratch=[
            pltpu.VMEM((width, width), BF16),
            pltpu.VMEM((width, hidden), BF16),
            pltpu.VMEM((rows, width), BF16),
            pltpu.VMEM((rows, width), BF16),
            pltpu.VMEM((2, 2 * keys, 2 * PAIR), BF16),
            pltpu.SemaphoreType.DMA((3,)),
            pltpu.SemaphoreType.DMA,
        ],
        far_outs=1,
    )
    (answers,) = run(
        answer,
        (shape((bricks * capacity, hidden), BF16),),
        near(asked),
        table,
        scratch=[
            pltpu.VMEM((bricks * capacity, hidden), BF16),
            pltpu.SemaphoreType.DMA((4,)),
        ],
        far_outs=1,
    )
    answers = lax.all_to_all(
        answers.reshape(bricks, capacity, hidden),
        ("gy", "gz"),
        split_axis=0,
        concat_axis=0,
        tiled=True,
    ).reshape(bricks * capacity, hidden)
    (part,) = run(
        own_part,
        (pltpu.VMEM((edges, hidden), F32),),
        edge_source.reshape(edges // 128, 128),
        node_state,
        w_source,
        contact,
        w_contact,
    )
    (scores,) = run(
        score, (shape((1, edges), F32),), place, near(answers), part, w_score.reshape(1, hidden)
    )
    return (node_state, scores.reshape(edges))


def solution(mesh):
    split = ("groups", "gy", "gz")
    in_specs = (
        P(split, None),
        P(split, None),
        P(split),
        P(split, None),
        P(split),
        P(split),
        P(split, None),
        P(),
        P(),
        P(),
        P(),
        P(),
        P(),
        P(),
    )
    out_specs = (P(split, None), P(split))
    return jax.shard_map(local, mesh=mesh, in_specs=in_specs, out_specs=out_specs, check_vma=False)
```
